32 devices in a mesh: groups: 2 (over y), pb: 4 (over x, core), ka: 4 (over z).
Axes of the slice: x: 2, y: 2, z: 4, core: 2. Of those that a mesh axis runs over, the one named last changes fastest.
Arguments:
- queries: bfloat16 [4096, 2048], P(('groups', 'pb')), parts along dimension 0, may hold values from -6 to 6
- keys: bfloat16 [4096, 2048], P(('groups', 'ka'), 'pb'), parts along dimension 0, may hold values from -6 to 6
- values: bfloat16 [4096, 2048], P(('groups', 'ka'), 'pb'), parts along dimension 0, may hold values from -6 to 6
- step_of: int32 [4096], P('groups'), parts along dimension 0, may hold values from 0 to 255, never falling along the last dimension, each value on 1 to 16 neighbouring positions
Outputs:
- attended: bfloat16 [4096, 2048], P(('groups', 'pb', 'ka')), parts along dimension 0
The draws below stay inside these ranges and needn't reach their ends.
There are 2 independent parts, one for each index of `groups`. The reference program is written for one: setup_inputs(seed, part) draws one part's arguments, and reference() takes and returns one part's arrays. A program takes and returns all parts, laid end to end along the dimension named above; each array names one. Nothing has to cross between parts.
Inputs may be any that keep to these rules, and one draw needn't show every extreme that they name: `step_of`: never falling along the episode; a step holds 1 to 16 tokens, one step exactly 16.
All inputs are finite; a program needn't handle non-finite values.
Results may differ from the reference program's by a relative error of at most 0.015.
Values may be sent and summed in bfloat16 or wider, within the bound.
A program may use at most 64 MiB of HBM per device.

```python
import math
import jax
import jax.numpy as jnp
import numpy as np
from jax import lax

HEADS = 16
HEAD_DIM = 128
MOST = 16
SEQ = 2048
STEPS = 256


def draw_queries(key, part):
    field_key = jax.random.fold_in(key, 1)
    field = 1.75 * jax.random.truncated_normal(field_key, -3.4, 3.4, (SEQ, HEADS * HEAD_DIM), jnp.float32)
    return field.astype(jnp.bfloat16)


def draw_keys(key, part):
    field_key = jax.random.fold_in(key, 2)
    field = 1.75 * jax.random.truncated_normal(field_key, -3.4, 3.4, (SEQ, HEADS * HEAD_DIM), jnp.float32)
    return field.astype(jnp.bfloat16)


def block_scale(key, dims, cuts, smallest, largest):
    loudness, own = 1.0, jax.random.fold_in(key, 6)
    for position, parts in cuts:
        draws = jnp.exp(jax.random.uniform(jax.random.fold_in(own, position), (parts,), jnp.float32, smallest / len(cuts), largest / len(cuts)))
        loudness = loudness * jnp.repeat(draws, dims[position] // parts).reshape([-1 if axis == position else 1 for axis in range(len(dims))])
    return loudness


def profile(count, total, bound, skew):
    loads = [(1 << 20) // math.isqrt(grade ** skew) + 1 for grade in range(2, count + 1)]
    rest, counts = total - bound - (count - 1), [1] * (count - 1)
    while rest > 0:
        candidates = [i for i in range(count - 1) if counts[i] < bound]
        pool, budget = sum([loads[i] for i in candidates]), rest
        for i in candidates:
            addition = min(bound - counts[i], max(1, budget * loads[i] // pool), rest)
            counts[i] = counts[i] + addition
            rest = rest - addition
    return np.array([bound] + counts)


def ragged_sizes(stream_key, count, total, limit, skew):
    if count == 2:
        one = jax.random.randint(stream_key, (), max(1, total - limit), min(limit, total - 1) + 1)
        return jnp.stack([one, total - one])
    lengths = jnp.asarray(profile(count, total, limit, skew), jnp.int32)
    pairs = (count - 1) // 2
    source_of, taker = lengths[1:1 + 2 * pairs:2], lengths[2:2 + 2 * pairs:2]
    slack = jnp.minimum(source_of - 1, limit - taker)
    moved = jax.random.randint(jax.random.fold_in(stream_key, 1), (pairs,), 0, 1 << 20) % (slack + 1)
    lengths = lengths.at[1:1 + 2 * pairs:2].set(source_of - moved).at[2:2 + 2 * pairs:2].set(taker + moved)
    return lengths[jax.random.permutation(jax.random.fold_in(stream_key, 2), count)]


def gaussian(rng, dims, scale, reach, split=(), held_as=jnp.bfloat16):
    values = jax.random.normal(rng, dims, jnp.float32) * scale
    if len(split) > 0:
        values = block_scale(rng, dims, split, -0.22, 0.18) * values
    return jnp.clip(values, min=-reach, max=reach).astype(held_as)


def setup_inputs(seed: int = 0, part: int = 0) -> dict:
    key_of = jax.random.split(jax.random.key(seed), 5)
    part_splits = jax.random.split(jax.random.fold_in(key_of[4], part), 5)
    return {
        "queries": draw_queries(jax.random.fold_in(jax.random.fold_in(key_of[4], part), 71), part),
        "keys": draw_keys(jax.random.fold_in(jax.random.fold_in(key_of[4], part), 71), part),
        "values": gaussian(part_splits[2], (SEQ, HEADS * HEAD_DIM), 1.0, 6.0, ((0, 4), (1, 4))),
        "step_of": jnp.searchsorted(jnp.cumsum(ragged_sizes(part_splits[3], STEPS, SEQ, MOST, 1)), jnp.arange(SEQ), side="right").astype(jnp.int32),
    }


def head_rows(q_rows, q_steps, keys_head, values_head, step_of):
    scores = jnp.dot(q_rows, keys_head.T, preferred_element_type=jnp.float32) * (1.0 / math.sqrt(HEAD_DIM))
    visible = step_of[None, :] <= q_steps[:, None]
    row_max = lax.optimization_barrier(jnp.max(jnp.where(visible, scores, -jnp.inf), axis=1, keepdims=True))
    weights = jnp.where(visible, jnp.exp(scores - row_max), 0.0)
    total = lax.optimization_barrier(jnp.sum(weights, axis=1, keepdims=True))
    mixed = jnp.dot(weights.astype(jnp.bfloat16), values_head, preferred_element_type=jnp.float32)
    return (mixed / total).astype(jnp.bfloat16)

def reference(queries, keys, values, step_of):
    block_rows = min(256, SEQ)
    block_count = SEQ // block_rows
    keys_heads = jnp.transpose(keys.reshape(SEQ, HEADS, HEAD_DIM), (1, 0, 2))
    values_heads = jnp.transpose(values.reshape(SEQ, HEADS, HEAD_DIM), (1, 0, 2))

    def one_block(index):
        start = (index * block_rows).astype(jnp.int32)
        q_rows = lax.dynamic_slice_in_dim(queries, start, block_rows, 0)
        q_steps = lax.dynamic_slice_in_dim(step_of, start, block_rows, 0)
        q_heads = jnp.transpose(q_rows.reshape(block_rows, HEADS, HEAD_DIM), (1, 0, 2))

        def one_head(head):
            return head_rows(q_heads[head], q_steps, keys_heads[head], values_heads[head], step_of)
        outputs = lax.map(one_head, jnp.arange(HEADS, dtype=jnp.int32))
        return jnp.transpose(outputs, (1, 0, 2)).reshape(block_rows, HEADS * HEAD_DIM)
    blocks = lax.map(one_block, jnp.arange(block_count, dtype=jnp.int32))
    return blocks.reshape(SEQ, HEADS * HEAD_DIM)
```

```python
import functools
import math

import jax
import jax.numpy as jnp
from jax import lax
from jax.experimental import pallas as pl
from jax.experimental.pallas import tpu as pltpu
from jax.sharding import PartitionSpec as P

HEAD_DIM = 128


LOW_SCORE = -1e30


def attend_half(q_rows, q_steps, keys_all, values_all, key_steps, block_keys):
    row_count, width = q_rows.shape
    head_size = HEAD_DIM
    head_count = width // head_size
    key_count = keys_all.shape[0]
    block_count = key_count // block_keys
    factor_scale = 1.0 / math.sqrt(head_size)
    q_heads = q_rows.reshape(row_count, head_count, head_size)
    blocks = (
        keys_all.reshape(block_count, block_keys, head_count, head_size),
        values_all.reshape(block_count, block_keys, head_count, head_size),
        key_steps.reshape(block_count, block_keys),
    )
    last_step = q_steps[row_count - 1]

    def compute(carry, key_block, value_block, step_block):
        run_max, run_sum, run_out = carry
        scores = (
            jnp.einsum("rhd,khd->hkr", q_heads, key_block, preferred_element_type=jnp.float32)
            * factor_scale
        )
        visible = step_block[None, :, None] <= q_steps[None, None, :]
        masked = jnp.where(visible, scores, LOW_SCORE)
        new_max = jnp.maximum(run_max, jnp.max(masked, axis=1))
        weights = jnp.where(visible, jnp.exp(masked - new_max[:, None, :]), 0.0)
        rescale = jnp.exp(run_max - new_max)
        new_sum = run_sum * rescale + jnp.sum(weights, axis=1)
        update = jnp.einsum(
            "hkr,khd->rhd",
            weights.astype(jnp.bfloat16),
            value_block,
            preferred_element_type=jnp.float32,
        )
        new_out = run_out * jnp.transpose(rescale)[:, :, None] + update
        return (new_max, new_sum, new_out)

    def visit(carry, block):
        key_block, value_block, step_block = block
        result = lax.cond(
            step_block[0] <= last_step,
            lambda state: compute(state, key_block, value_block, step_block),
            lambda state: state,
            carry,
        )
        return (result, None)

    initial = (
        jnp.full((head_count, row_count), LOW_SCORE, jnp.float32),
        jnp.zeros((head_count, row_count), jnp.float32),
        jnp.zeros((row_count, head_count, head_size), jnp.float32),
    )
    final_state, unused = lax.scan(visit, initial, blocks)
    return final_state


def on_device_blocks(queries, keys, values, step_of):
    block_rows, width = queries.shape
    head_size = HEAD_DIM
    head_count = width // head_size
    key_parts = lax.axis_size("ka")
    query_index = lax.axis_index("pb")
    key_index = lax.axis_index("ka")
    shard_rows = block_rows // key_parts
    half_rows = block_rows // 2
    key_count = keys.shape[0]
    first_steps = lax.dynamic_slice_in_dim(step_of, query_index * block_rows, half_rows)
    second_steps = lax.dynamic_slice_in_dim(
        step_of, query_index * block_rows + half_rows, half_rows
    )
    keys_mine, values_mine = (keys, values)
    key_steps = lax.dynamic_slice_in_dim(step_of, key_index * key_count, key_count)
    keys_all, values_all = (
        lax.all_gather(keys_mine, "pb", axis=1, tiled=True),
        lax.all_gather(values_mine, "pb", axis=1, tiled=True),
    )
    block_keys = math.gcd(64, key_count)
    first_state = attend_half(
        queries[:half_rows], first_steps, keys_all, values_all, key_steps, block_keys
    )
    second_state = attend_half(
        queries[half_rows:], second_steps, keys_all, values_all, key_steps, block_keys
    )
    row_max = jnp.concatenate([first_state[0], second_state[0]], axis=1)
    row_sum = jnp.concatenate([first_state[1], second_state[1]], axis=1)
    row_out = jnp.concatenate([first_state[2], second_state[2]], axis=0)
    sent = (
        jnp.transpose(row_max)[:, None, :],
        jnp.transpose(row_sum)[:, None, :],
        row_out.reshape(block_rows, 1, width),
    )
    got_max, got_sum, got_out = (
        lax.all_to_all(sent[0], "ka", split_axis=0, concat_axis=1, tiled=True),
        lax.all_to_all(sent[1], "ka", split_axis=0, concat_axis=1, tiled=True),
        lax.all_to_all(sent[2], "ka", split_axis=0, concat_axis=1, tiled=True),
    )
    best = jnp.max(got_max, axis=1, keepdims=True)
    weight = jnp.exp(got_max - best)
    total = jnp.sum(got_sum * weight, axis=1)
    shares = weight / total[:, None, :]
    pieces = got_out.reshape(shard_rows, key_parts, head_count, head_size) * shares[:, :, :, None]
    result = jnp.sum(pieces, axis=1).reshape(shard_rows, width)
    result = result.astype(jnp.bfloat16)
    return result


MOST = 16
MESH = pl.DeviceIdType.MESH


def head_kernel(
    parts_q, parts_k, block_q, q_ref, k_ref, v_ref, step_ref, out_ref,
    qbuf, kbuf, vbuf, obuf, pbuf,
    q_send, k_send, v_send, o_send, q_recv, k_recv, v_recv, o_recv, ready,
    step_buf, step_sem,
):
    head_size = HEAD_DIM
    p, a = lax.axis_index("pb"), lax.axis_index("ka")
    me = p * parts_k + a
    devices = parts_q * parts_k
    q_rows, k_rows = q_ref.shape[0], k_ref.shape[0]
    o_rows = out_ref.shape[0]
    seq = qbuf.shape[0]
    factor = math.log2(math.e) / math.sqrt(head_size)

    relay = parts_k - 1
    barrier = pltpu.get_barrier_semaphore()

    def signal(sem, to_p, to_a):
        pl.semaphore_signal(
            sem, inc=1, device_id={"pb": to_p, "ka": to_a}, device_id_type=MESH
        )

    for d in range(1, parts_k):
        signal(barrier, p, lax.rem(a + d, parts_k))

    @pl.when(a == relay)
    def _():
        for d in range(1, parts_q):
            signal(barrier, lax.rem(p + d, parts_q), relay)

    @pl.when(a != relay)
    def _():
        pl.semaphore_wait(barrier, parts_k - 1)

    @pl.when(a == relay)
    def _():
        pl.semaphore_wait(barrier, parts_k + parts_q - 2)
        for d in range(1, parts_q):
            signal(ready.at[p], lax.rem(p + d, parts_q), relay)

    def head_columns(index):
        return pl.ds(pl.multiple_of(index * head_size, head_size), head_size)

    k_place = pl.ds(pl.multiple_of(a * k_rows, k_rows), k_rows)
    q_place = pl.ds(pl.multiple_of(p * q_rows, q_rows), q_rows)

    own = [
        (k_ref.at[:, head_columns(a)], kbuf.at[k_place], k_recv.at[a]),
        (v_ref.at[:, head_columns(a)], vbuf.at[k_place], v_recv.at[a]),
        (q_ref.at[:, head_columns(me)], qbuf.at[q_place], q_recv.at[p]),
    ]
    for source, target, sem in own:
        pltpu.make_async_copy(source, target, sem).start()
    pltpu.make_async_copy(step_ref, step_buf, step_sem).start()
    sends = []

    def send(source, target, send_sem, recv_sem, to_p, to_a):
        copy = pltpu.make_async_remote_copy(
            src_ref=source, dst_ref=target, send_sem=send_sem, recv_sem=recv_sem,
            device_id={"pb": to_p, "ka": to_a}, device_id_type=MESH,
        )
        copy.start()
        sends.append(copy)

    for d in range(parts_k - 1, 0, -1):
        to = a
        for bit in range(d.bit_length()):
            if d >> bit & 1:
                to += (1 - 2 * lax.rem(a // 2 ** bit, 2)) * 2 ** bit
        send(
            k_ref.at[:, head_columns(to)], kbuf.at[k_place],
            k_send.at[d - 1], k_recv.at[a], p, to,
        )
    for d in range(parts_k - 1, 0, -1):
        to = a
        for bit in range(d.bit_length()):
            if d >> bit & 1:
                to += (1 - 2 * lax.rem(a // 2 ** bit, 2)) * 2 ** bit
        send(
            v_ref.at[:, head_columns(to)], vbuf.at[k_place],
            v_send.at[d - 1], v_recv.at[a], p, to,
        )

    for to in reversed(range(parts_q)):
        @pl.when(p != to)
        def _():
            pl.semaphore_wait(ready.at[to], 1)

            @pl.when(a == relay)
            def _():
                for other in range(parts_k - 1):
                    signal(ready.at[to], p, other)

            pltpu.make_async_remote_copy(
                src_ref=q_ref.at[:, head_columns(to * parts_k + a)],
                dst_ref=qbuf.at[q_place],
                send_sem=q_send.at[to], recv_sem=q_recv.at[p],
                device_id={"pb": to, "ka": a}, device_id_type=MESH,
            ).start()

    def arrived(buffer, rows, sem, index):
        block = buffer.at[index * rows:(index + 1) * rows]
        pltpu.make_async_copy(block, block, sem.at[index]).wait()

    pltpu.make_async_copy(step_ref, step_buf, step_sem).wait()
    steps = step_buf[...].astype(jnp.float32)
    have_q = have_k = 0
    blocks = [
        (start, start + block_q, min(start + block_q + 128, seq))
        for start in range(0, seq, block_q)
    ]
    totals = []
    for start, stop, key_stop in blocks:
        while have_q * q_rows < stop:
            arrived(qbuf, q_rows, q_recv, have_q)
            have_q += 1
        while have_k * k_rows < key_stop:
            arrived(kbuf, k_rows, k_recv, have_k)
            have_k += 1
        q_block = qbuf[start:stop, :]
        q_steps = jnp.concatenate(
            [
                jnp.transpose(jnp.broadcast_to(steps[:, row:row + 128], (128, 128)))
                for row in range(start, stop, 128)
            ],
            axis=0,
        )
        pieces = []
        if start > 0:
            pieces.append((0, start))
        pieces.append((start, key_stop))
        scores = []
        for low, high in pieces:
            score = lax.dot_general(
                q_block, kbuf[low:high, :], (((1,), (1,)), ((), ())),
                preferred_element_type=jnp.float32,
            )
            if high > start:
                visible = jnp.concatenate(
                    [
                        steps[:, row:row + 128] <= q_steps
                        for row in range(low, high, 128)
                    ],
                    axis=1,
                )
                score = jnp.where(visible, score, LOW_SCORE)
            scores.append(score)
        row_max = jnp.max(scores[0], axis=1, keepdims=True)
        for score in scores[1:]:
            row_max = jnp.maximum(row_max, jnp.max(score, axis=1, keepdims=True))
        total = None
        for (low, high), score in zip(pieces, scores):
            weights = jnp.exp2((score - row_max) * factor)
            part = jnp.sum(weights, axis=1, keepdims=True)
            pbuf[start:stop, low:high] = weights.astype(jnp.bfloat16)
            total = part if total is None else total + part
        totals.append(total)

    have_k = 0
    for (start, stop, key_stop), total in zip(blocks, totals):
        while have_k * k_rows < key_stop:
            arrived(vbuf, k_rows, v_recv, have_k)
            have_k += 1
        mixed = jnp.dot(
            pbuf[start:stop, :key_stop], vbuf[:key_stop, :],
            preferred_element_type=jnp.float32,
        )
        obuf[start:stop, :] = (mixed / total).astype(jnp.bfloat16)
        for shard in range(start // o_rows, stop // o_rows):
            source = obuf.at[shard * o_rows:(shard + 1) * o_rows]
            target = out_ref.at[:, head_columns(me)]

            @pl.when(me == shard)
            def _():
                pltpu.make_async_copy(source, target, o_recv.at[me]).start()

            @pl.when(me != shard)
            def _():
                pltpu.make_async_remote_copy(
                    src_ref=source, dst_ref=target,
                    send_sem=o_send.at[shard], recv_sem=o_recv.at[me],
                    device_id={"pb": shard // parts_k, "ka": shard % parts_k},
                    device_id_type=MESH,
                ).start()

    for copy in sends:
        copy.wait_send()
    for to in range(parts_q):
        @pl.when(p != to)
        def _():
            pltpu.make_async_copy(
                qbuf.at[:q_rows], qbuf.at[:q_rows], q_send.at[to]
            ).wait()

    for shard in range(devices):
        block = obuf.at[shard * o_rows:(shard + 1) * o_rows]

        @pl.when(me != shard)
        def _():
            pltpu.make_async_copy(block, block, o_send.at[shard]).wait()

        piece = out_ref.at[:, shard * head_size:(shard + 1) * head_size]
        pltpu.make_async_copy(piece, piece, o_recv.at[shard]).wait()


def on_device_heads(queries, keys, values, step_of):
    parts_q, parts_k = lax.axis_size("pb"), lax.axis_size("ka")
    block_rows, width = queries.shape
    seq = step_of.shape[0]
    shard_rows = block_rows // parts_k
    devices = parts_q * parts_k
    block_q = max(256, shard_rows)
    buffer = pltpu.VMEM((seq, HEAD_DIM), jnp.bfloat16)
    anywhere = pl.BlockSpec(memory_space=pltpu.HBM)
    return pl.pallas_call(
        functools.partial(head_kernel, parts_q, parts_k, block_q),
        out_shape=jax.ShapeDtypeStruct((shard_rows, width), jnp.bfloat16),
        in_specs=[anywhere, anywhere, anywhere, anywhere],
        out_specs=pl.BlockSpec(memory_space=pltpu.VMEM),
        scratch_shapes=[
            buffer, buffer, buffer, buffer,
            pltpu.VMEM((seq, seq), jnp.bfloat16),
            pltpu.SemaphoreType.DMA((parts_q,)),
            pltpu.SemaphoreType.DMA((parts_k - 1,)),
            pltpu.SemaphoreType.DMA((parts_k - 1,)),
            pltpu.SemaphoreType.DMA((devices,)),
            pltpu.SemaphoreType.DMA((parts_q,)),
            pltpu.SemaphoreType.DMA((parts_k,)),
            pltpu.SemaphoreType.DMA((parts_k,)),
            pltpu.SemaphoreType.DMA((devices,)),
            pltpu.SemaphoreType.REGULAR((parts_q,)),
            pltpu.VMEM((1, seq), jnp.int32),
            pltpu.SemaphoreType.DMA,
        ],
        compiler_params=pltpu.CompilerParams(
            collective_id=0, has_side_effects=True, vmem_limit_bytes=40 * 1024 * 1024
        ),
    )(*[
        pltpu.with_memory_space_constraint(array, pltpu.HBM)
        for array in (queries, keys, values, step_of.reshape(1, seq))
    ])


def head_per_device(mesh_shape, queries, keys, step_of):
    parts_q, parts_k = mesh_shape["pb"], mesh_shape["ka"]
    shard_rows = queries.shape[0] // parts_k
    return (
        keys.shape[1] == parts_k * HEAD_DIM
        and parts_q > 1
        and parts_k > 1
        and shard_rows % 128 == 0
        and step_of.shape[0] % max(256, shard_rows) == 0
        and (256 % shard_rows == 0 or shard_rows % 256 == 0)
    )


def solution(mesh):
    placed = (
        P(("groups", "pb"), None),
        P(("groups", "ka"), "pb"),
        P(("groups", "ka"), "pb"),
        P("groups"),
    )

    def on_device(queries, keys, values, step_of):
        if head_per_device(mesh.shape, queries, keys, step_of):
            return on_device_heads(queries, keys, values, step_of)
        return on_device_blocks(queries, keys, values, step_of)

    return jax.shard_map(
        on_device,
        mesh=mesh,
        in_specs=placed,
        out_specs=P(("groups", "pb", "ka"), None),
        check_vma=False,
    )
```

```python
import functools
import math

import jax
import jax.numpy as jnp
from jax import lax
from jax.experimental import pallas as pl
from jax.experimental.pallas import tpu as pltpu
from jax.sharding import PartitionSpec as P

HEAD_DIM = 128


LOW_SCORE = -1e30


def attend_half(q_rows, q_steps, keys_all, values_all, key_steps, block_keys):
    row_count, width = q_rows.shape
    head_size = HEAD_DIM
    head_count = width // head_size
    key_count = keys_all.shape[0]
    block_count = key_count // block_keys
    factor_scale = 1.0 / math.sqrt(head_size)
    q_heads = q_rows.reshape(row_count, head_count, head_size)
    blocks = (
        keys_all.reshape(block_count, block_keys, head_count, head_size),
        values_all.reshape(block_count, block_keys, head_count, head_size),
        key_steps.reshape(block_count, block_keys),
    )
    last_step = q_steps[row_count - 1]

    def compute(carry, key_block, value_block, step_block):
        run_max, run_sum, run_out = carry
        scores = (
            jnp.einsum("rhd,khd->hkr", q_heads, key_block, preferred_element_type=jnp.float32)
            * factor_scale
        )
        visible = step_block[None, :, None] <= q_steps[None, None, :]
        masked = jnp.where(visible, scores, LOW_SCORE)
        new_max = jnp.maximum(run_max, jnp.max(masked, axis=1))
        weights = jnp.where(visible, jnp.exp(masked - new_max[:, None, :]), 0.0)
        rescale = jnp.exp(run_max - new_max)
        new_sum = run_sum * rescale + jnp.sum(weights, axis=1)
        update = jnp.einsum(
            "hkr,khd->rhd",
            weights.astype(jnp.bfloat16),
            value_block,
            preferred_element_type=jnp.float32,
        )
        new_out = run_out * jnp.transpose(rescale)[:, :, None] + update
        return (new_max, new_sum, new_out)

    def visit(carry, block):
        key_block, value_block, step_block = block
        result = lax.cond(
            step_block[0] <= last_step,
            lambda state: compute(state, key_block, value_block, step_block),
            lambda state: state,
            carry,
        )
        return (result, None)

    initial = (
        jnp.full((head_count, row_count), LOW_SCORE, jnp.float32),
        jnp.zeros((head_count, row_count), jnp.float32),
        jnp.zeros((row_count, head_count, head_size), jnp.float32),
    )
    final_state, unused = lax.scan(visit, initial, blocks)
    return final_state


def on_device_blocks(queries, keys, values, step_of):
    block_rows, width = queries.shape
    head_size = HEAD_DIM
    head_count = width // head_size
    key_parts = lax.axis_size("ka")
    query_index = lax.axis_index("pb")
    key_index = lax.axis_index("ka")
    shard_rows = block_rows // key_parts
    half_rows = block_rows // 2
    key_count = keys.shape[0]
    first_steps = lax.dynamic_slice_in_dim(step_of, query_index * block_rows, half_rows)
    second_steps = lax.dynamic_slice_in_dim(
        step_of, query_index * block_rows + half_rows, half_rows
    )
    keys_mine, values_mine = (keys, values)
    key_steps = lax.dynamic_slice_in_dim(step_of, key_index * key_count, key_count)
    keys_all, values_all = (
        lax.all_gather(keys_mine, "pb", axis=1, tiled=True),
        lax.all_gather(values_mine, "pb", axis=1, tiled=True),
    )
    block_keys = math.gcd(64, key_count)
    first_state = attend_half(
        queries[:half_rows], first_steps, keys_all, values_all, key_steps, block_keys
    )
    second_state = attend_half(
        queries[half_rows:], second_steps, keys_all, values_all, key_steps, block_keys
    )
    row_max = jnp.concatenate([first_state[0], second_state[0]], axis=1)
    row_sum = jnp.concatenate([first_state[1], second_state[1]], axis=1)
    row_out = jnp.concatenate([first_state[2], second_state[2]], axis=0)
    sent = (
        jnp.transpose(row_max)[:, None, :],
        jnp.transpose(row_sum)[:, None, :],
        row_out.reshape(block_rows, 1, width),
    )
    got_max, got_sum, got_out = (
        lax.all_to_all(sent[0], "ka", split_axis=0, concat_axis=1, tiled=True),
        lax.all_to_all(sent[1], "ka", split_axis=0, concat_axis=1, tiled=True),
        lax.all_to_all(sent[2], "ka", split_axis=0, concat_axis=1, tiled=True),
    )
    best = jnp.max(got_max, axis=1, keepdims=True)
    weight = jnp.exp(got_max - best)
    total = jnp.sum(got_sum * weight, axis=1)
    shares = weight / total[:, None, :]
    pieces = got_out.reshape(shard_rows, key_parts, head_count, head_size) * shares[:, :, :, None]
    result = jnp.sum(pieces, axis=1).reshape(shard_rows, width)
    result = result.astype(jnp.bfloat16)
    return result


PARTS = 4
MESH = pl.DeviceIdType.MESH


def head_kernel(
    q_ref, k_ref, v_ref, step_ref, out_ref,
    qbuf, kbuf, vbuf, obuf, pbuf, held, held_lse, part_out, part_in, lse_out, lse_in, step_buf,
    q_send, k_send, v_send, o_send, part_send, lse_send,
    q_recv, k_recv, v_recv, o_recv, part_recv, lse_recv, step_sem,
    ready, entered_q, entered_k,
):
    head_size = HEAD_DIM
    parts_q = parts_k = PARTS
    p, a = lax.axis_index("pb"), lax.axis_index("ka")
    me = p * parts_k + a
    q_rows, k_rows = q_ref.shape[0], k_ref.shape[0]
    o_rows = out_ref.shape[0]
    seq = qbuf.shape[1]
    half = seq // 2
    block = 2 * o_rows
    factor = math.log2(math.e) / math.sqrt(head_size)
    barrier = pltpu.get_barrier_semaphore()

    def signal(sem, to_p, to_a):
        pl.semaphore_signal(
            sem, inc=1, device_id={"pb": to_p, "ka": to_a}, device_id_type=MESH
        )

    for other in range(1, parts_k):
        @pl.when(other > a)
        def _():
            signal(barrier, p, other)

    for other in range(1, parts_q):
        @pl.when(other > p)
        def _():
            signal(barrier, other, a)

    @pl.when(a + p > 0)
    def _():
        pl.semaphore_wait(barrier, a + p)

    for other in range(parts_k - 1):
        @pl.when(other < a)
        def _():
            signal(entered_k.at[a], p, other)

    for other in range(parts_q - 1):
        @pl.when(other < p)
        def _():
            signal(entered_q.at[p], other, a)

    def head_columns(index):
        return pl.ds(pl.multiple_of(index * head_size, head_size), head_size)

    q_place = pl.ds(pl.multiple_of(p * q_rows, q_rows), q_rows)

    def keys_of(layer, local, slot):
        place = slice(layer * k_rows, (layer + 1) * k_rows)
        column = slice(local * head_size, (local + 1) * head_size)
        for source, target, sem in ((k_ref, kbuf, k_recv), (v_ref, vbuf, v_recv)):
            pltpu.make_async_copy(
                source.at[:, column], target.at[slot, place], sem.at[slot, layer]
            ).start()

    def send_keys(layer, local, slot, to, rows=None):
        rows = k_rows if rows is None else rows
        place = slice(layer * k_rows, layer * k_rows + rows)
        column = slice(local * head_size, (local + 1) * head_size)
        for source, target, sent, sem in (
            (k_ref, kbuf, k_send, k_recv), (v_ref, vbuf, v_send, v_recv)
        ):
            pltpu.make_async_remote_copy(
                src_ref=source.at[:rows, column], dst_ref=target.at[slot, place],
                send_sem=sent.at[local], recv_sem=sem.at[slot, layer],
                device_id={"pb": p, "ka": to}, device_id_type=MESH,
            ).start()

    def wait_keys_sent(local, rows):
        for source, sent in ((kbuf, k_send), (vbuf, v_send)):
            piece = source.at[0, :rows]
            pltpu.make_async_copy(piece, piece, sent.at[local]).wait()

    @pl.when(a == 0)
    def _():
        keys_of(0, 0, 0)
        pl.semaphore_wait(entered_k.at[1], 1)
        send_keys(0, 1, 0, 1)
        pl.semaphore_wait(entered_k.at[3], 1)
        send_keys(0, 3, 0, 3)
        send_keys(0, 2, 1, 1)
        pl.semaphore_wait(entered_k.at[2], 1)

    @pl.when(a == 1)
    def _():
        keys_of(1, 1, 0)
        pl.semaphore_wait(entered_k.at[3], 1)
        send_keys(1, 3, 0, 3)
        send_keys(1, 0, 0, 0)
        keys_of(1, 2, 1)
        pl.semaphore_wait(entered_k.at[2], 1)

    @pl.when(a == 2)
    def _():
        keys_of(2, 1, 0)
        send_keys(2, 0, 0, 0)
        send_keys(2, 1, 0, 1, o_rows)
        pl.semaphore_wait(entered_k.at[3], 1)
        send_keys(2, 3, 0, 3)
        send_keys(2, 2, 1, 1, o_rows)
        keys_of(2, 2, 1)

    @pl.when(a == 3)
    def _():
        send_keys(3, 1, 0, 2)
        send_keys(3, 0, 0, 0)
        send_keys(3, 2, 1, 2)
        keys_of(3, 3, 0)

    step_copy = pltpu.make_async_copy(step_ref, step_buf, step_sem)
    step_copy.start()

    split = jnp.logical_or(a == 1, a == 2)
    sends_q = jnp.logical_or(a != 2, p >= parts_q // 2)

    for to in reversed(range(parts_q)):
        @pl.when(p != to)
        def _():
            @pl.when(to > p)
            def _():
                pl.semaphore_wait(entered_q.at[to], 1)

            signal(ready.at[p], to, a)

    def send_queries(slot, local):
        for to in reversed(range(parts_q)):
            source = q_ref.at[:, head_columns(to * parts_k + local)]

            @pl.when(p != to)
            def _():
                pltpu.make_async_remote_copy(
                    src_ref=source, dst_ref=qbuf.at[slot, q_place],
                    send_sem=q_send.at[slot, to], recv_sem=q_recv.at[slot, p],
                    device_id={"pb": to, "ka": a}, device_id_type=MESH,
                ).start()

            @pl.when(p == to)
            def _():
                pltpu.make_async_copy(
                    source, qbuf.at[slot, q_place], q_recv.at[slot, p]
                ).start()

    @pl.when(sends_q)
    def _():
        send_queries(0, jnp.where(split, 1, a))

    @pl.when(jnp.logical_and(sends_q, split))
    def _():
        send_queries(1, 2)

    step_copy.wait()
    steps = step_buf[...].astype(jnp.float32)
    for other in range(parts_q):
        @pl.when(p != other)
        def _():
            pl.semaphore_wait(ready.at[other], 1)

    def arrived(piece, sem):
        pltpu.make_async_copy(piece, piece, sem).wait()

    def queries_in(slot, part):
        arrived(qbuf.at[slot, part * q_rows:(part + 1) * q_rows], q_recv.at[slot, part])

    def keys_in(slot, layer, rows=None):
        rows = k_rows if rows is None else rows
        place = slice(layer * k_rows, layer * k_rows + rows)
        arrived(kbuf.at[slot, place], k_recv.at[slot, layer])
        arrived(vbuf.at[slot, place], v_recv.at[slot, layer])

    def attend(slot, start, low, middle, high):
        stop = start + block
        q_block = qbuf[slot, start:stop, :]
        pieces = [(one, two) for one, two in ((low, middle), (middle, high)) if two > one]
        scores = []
        for one, two in pieces:
            score = lax.dot_general(
                q_block, kbuf[slot, one:two, :], (((1,), (1,)), ((), ())),
                preferred_element_type=jnp.float32,
            )
            if one >= middle:
                q_steps = jnp.concatenate(
                    [
                        jnp.transpose(jnp.broadcast_to(steps[:, row:row + 128], (128, 128)))
                        for row in range(start, stop, 128)
                    ],
                    axis=0,
                )
                visible = jnp.concatenate(
                    [steps[:, row:row + 128] <= q_steps for row in range(one, two, 128)],
                    axis=1,
                )
                score = jnp.where(visible, score, LOW_SCORE)
            scores.append(score)
        row_max = jnp.max(scores[0], axis=1, keepdims=True)
        for score in scores[1:]:
            row_max = jnp.maximum(row_max, jnp.max(score, axis=1, keepdims=True))
        total = None
        for (one, two), score in zip(pieces, scores):
            weights = jnp.exp2((score - row_max) * factor)
            part = jnp.sum(weights, axis=1, keepdims=True)
            pbuf[start:stop, one:two] = weights.astype(jnp.bfloat16)
            total = part if total is None else total + part
        mixed = jnp.dot(
            pbuf[start:stop, low:high], vbuf[slot, low:high, :],
            preferred_element_type=jnp.float32,
        )
        return mixed / total, row_max * factor + jnp.log2(total)

    def deliver(slot, head, start, result):
        obuf[slot, start:start + block, :] = result.astype(jnp.bfloat16)
        for shard in range(start // o_rows, (start + block) // o_rows):
            source = obuf.at[slot, shard * o_rows:(shard + 1) * o_rows]
            target = out_ref.at[:, head_columns(head)]

            @pl.when(me == shard)
            def _():
                pltpu.make_async_copy(source, target, o_recv.at[head]).start()

            @pl.when(me != shard)
            def _():
                pltpu.make_async_remote_copy(
                    src_ref=source, dst_ref=target,
                    send_sem=o_send.at[slot, shard], recv_sem=o_recv.at[head],
                    device_id={"pb": shard // parts_k, "ka": shard % parts_k},
                    device_id_type=MESH,
                ).start()

    def delivered(slot, starts):
        for start in starts:
            for shard in range(start // o_rows, (start + block) // o_rows):
                @pl.when(me != shard)
                def _():
                    arrived(
                        obuf.at[slot, shard * o_rows:(shard + 1) * o_rows],
                        o_send.at[slot, shard],
                    )

    def part_copies(slot, index, to):
        return [
            pltpu.make_async_remote_copy(
                src_ref=source.at[slot, index], dst_ref=target.at[slot, index],
                send_sem=sent.at[slot, index], recv_sem=sem.at[slot, index],
                device_id={"pb": p, "ka": to}, device_id_type=MESH,
            )
            for source, target, sent, sem in (
                (part_out, part_in, part_send, part_recv), (lse_out, lse_in, lse_send, lse_recv)
            )
        ]

    def pass_on(slot, index, to, result, lse):
        part_out[slot, index] = result.astype(jnp.bfloat16)
        for i in range(block // 128):
            row = jnp.transpose(jnp.broadcast_to(lse[i * 128:(i + 1) * 128], (128, 128)))
            lse_out[slot, index, i * 8:(i + 1) * 8, :] = row[:8]
        for copy in part_copies(slot, index, to):
            copy.start()

    def hold(slot, index, result, lse):
        held[slot, index] = result
        held_lse[slot, index] = jnp.broadcast_to(lse, (block, 128))

    def merged(slot, index, to):
        for copy in part_copies(slot, index, to):
            copy.wait_recv()
        other_lse = jnp.concatenate(
            [
                jnp.transpose(
                    jnp.broadcast_to(lse_in[slot, index, i * 8:i * 8 + 1, :], (128, 128))
                )
                for i in range(block // 128)
            ],
            axis=0,
        )
        mine_lse = held_lse[slot, index]
        best = jnp.maximum(mine_lse, other_lse)
        mine, other = jnp.exp2(mine_lse - best), jnp.exp2(other_lse - best)
        both = held[slot, index] * mine + part_in[slot, index].astype(jnp.float32) * other
        return both / (mine + other)

    low_side = [half, half + 2 * block]
    high_side = [half + block, half + 3 * block]

    @pl.when(jnp.logical_not(split))
    def _():
        have_q = have_k = 0
        for start in range(0, seq, block):
            stop = start + block
            high = min(stop + 128, seq)
            while have_q * q_rows < stop:
                queries_in(0, have_q)
                have_q += 1
            while have_k * k_rows < high:
                keys_in(0, have_k)
                have_k += 1
            result, unused = attend(0, start, 0, start, high)
            deliver(0, p * parts_k + a, start, result)
        delivered(0, range(0, seq, block))

    @pl.when(a == 1)
    def _():
        def one_head(slot, carry):
            head = p * parts_k + 1 + slot
            keys_in(slot, 1)
            for part in (2, 3):
                queries_in(slot, part)
            keys_in(slot, 0)
            for index, start in enumerate(high_side):
                pass_on(slot, index, 2, *attend(slot, start, 0, half, half))
            for part in (0, 1):
                queries_in(slot, part)
            keys_in(slot, 2, o_rows)
            for start in (3 * block, block, 2 * block, 0):
                result, unused = attend(slot, start, 0, start, start + block + 128)
                deliver(slot, head, start, result)
            for index, start in enumerate(low_side):
                hold(slot, index, *attend(slot, start, 0, half, half))
            for index, start in enumerate(low_side):
                deliver(slot, head, start, merged(slot, index, 2))
            return carry

        lax.fori_loop(0, 2, one_head, 0)
        for slot in range(2):
            for index in range(2):
                for copy in part_copies(slot, index, 2):
                    copy.wait_send()
            delivered(slot, [*range(0, half, block), *low_side])

    @pl.when(a == 2)
    def _():
        def one_head(slot, carry):
            keys_in(slot, 2)
            queries_in(slot, 2)
            queries_in(slot, 3)
            keys_in(slot, 3)
            for index, start in enumerate(low_side):
                pass_on(slot, index, 1, *attend(slot, start, half, start, start + block + 128))
            for index, start in enumerate(high_side):
                high = min(start + block + 128, seq)
                hold(slot, index, *attend(slot, start, half, start, high))
            return carry

        def merge_head(slot, carry):
            head = p * parts_k + 1 + slot
            for index, start in enumerate(high_side):
                deliver(slot, head, start, merged(slot, index, 1))
            return carry

        lax.fori_loop(0, 2, one_head, 0)
        lax.fori_loop(0, 2, merge_head, 0)
        for slot in range(2):
            for index in range(2):
                for copy in part_copies(slot, index, 1):
                    copy.wait_send()
            delivered(slot, high_side)

    for layer, sent in enumerate((
        ((1, k_rows), (3, k_rows), (2, k_rows)),
        ((3, k_rows), (0, k_rows)),
        ((0, k_rows), (1, o_rows), (3, k_rows), (2, o_rows)),
        ((1, k_rows), (0, k_rows), (2, k_rows)),
    )):
        @pl.when(a == layer)
        def _():
            for local, rows in sent:
                wait_keys_sent(local, rows)

    def wait_queries_sent(slot):
        for to in range(parts_q):
            @pl.when(p != to)
            def _():
                arrived(qbuf.at[slot, :q_rows], q_send.at[slot, to])

    @pl.when(sends_q)
    def _():
        wait_queries_sent(0)

    @pl.when(jnp.logical_and(sends_q, split))
    def _():
        wait_queries_sent(1)

    for head in range(parts_q * parts_k):
        arrived(out_ref.at[:, head * head_size:(head + 1) * head_size], o_recv.at[head])


def on_device_heads(queries, keys, values, step_of):
    block_rows, width = queries.shape
    seq = step_of.shape[0]
    shard_rows = block_rows // PARTS
    block = 2 * shard_rows
    buffer = pltpu.VMEM((2, seq, HEAD_DIM), jnp.bfloat16)
    anywhere = pl.BlockSpec(memory_space=pltpu.HBM)
    dma = pltpu.SemaphoreType.DMA
    return pl.pallas_call(
        head_kernel,
        out_shape=jax.ShapeDtypeStruct((shard_rows, width), jnp.bfloat16),
        in_specs=[anywhere, anywhere, anywhere, anywhere],
        out_specs=pl.BlockSpec(memory_space=pltpu.VMEM),
        scratch_shapes=[
            buffer, buffer, buffer, buffer,
            pltpu.VMEM((seq, seq), jnp.bfloat16),
            pltpu.VMEM((2, 2, block, HEAD_DIM), jnp.float32),
            pltpu.VMEM((2, 2, block, HEAD_DIM), jnp.float32),
            pltpu.VMEM((2, 2, block, HEAD_DIM), jnp.bfloat16),
            pltpu.VMEM((2, 2, block, HEAD_DIM), jnp.bfloat16),
            pltpu.VMEM((2, 2, block // 16, 128), jnp.float32),
            pltpu.VMEM((2, 2, block // 16, 128), jnp.float32),
            pltpu.VMEM((1, seq), jnp.int32),
            dma((2, PARTS)), dma((PARTS,)), dma((PARTS,)), dma((2, PARTS * PARTS)),
            dma((2, 2)), dma((2, 2)),
            dma((2, PARTS)), dma((2, PARTS)), dma((2, PARTS)), dma((PARTS * PARTS,)),
            dma((2, 2)), dma((2, 2)), dma,
            pltpu.SemaphoreType.REGULAR((PARTS,)),
            pltpu.SemaphoreType.REGULAR((PARTS,)),
            pltpu.SemaphoreType.REGULAR((PARTS,)),
        ],
        compiler_params=pltpu.CompilerParams(
            collective_id=0, has_side_effects=True, vmem_limit_bytes=48 * 1024 * 1024
        ),
    )(*[
        pltpu.with_memory_space_constraint(array, pltpu.HBM)
        for array in (queries, keys, values, step_of.reshape(1, seq))
    ])


def head_per_device(mesh_shape, queries, keys, step_of):
    return (
        mesh_shape["pb"] == PARTS
        and mesh_shape["ka"] == PARTS
        and keys.shape[1] == PARTS * HEAD_DIM
        and step_of.shape[0] == PARTS * PARTS * 128
    )


def solution(mesh):
    placed = (
        P(("groups", "pb"), None),
        P(("groups", "ka"), "pb"),
        P(("groups", "ka"), "pb"),
        P("groups"),
    )

    def on_device(queries, keys, values, step_of):
        if head_per_device(mesh.shape, queries, keys, step_of):
            return on_device_heads(queries, keys, values, step_of)
        return on_device_blocks(queries, keys, values, step_of)

    return jax.shard_map(
        on_device,
        mesh=mesh,
        in_specs=placed,
        out_specs=P(("groups", "pb", "ka"), None),
        check_vma=False,
    )
```

```python
import functools
import math

import jax
import jax.numpy as jnp
from jax import lax
from jax.experimental import pallas as pl
from jax.experimental.pallas import tpu as pltpu
from jax.sharding import PartitionSpec as P

HEAD_DIM = 128


LOW_SCORE = -1e30


def attend_half(q_rows, q_steps, keys_all, values_all, key_steps, block_keys):
    row_count, width = q_rows.shape
    head_size = HEAD_DIM
    head_count = width // head_size
    key_count = keys_all.shape[0]
    block_count = key_count // block_keys
    factor_scale = 1.0 / math.sqrt(head_size)
    q_heads = q_rows.reshape(row_count, head_count, head_size)
    blocks = (
        keys_all.reshape(block_count, block_keys, head_count, head_size),
        values_all.reshape(block_count, block_keys, head_count, head_size),
        key_steps.reshape(block_count, block_keys),
    )
    last_step = q_steps[row_count - 1]

    def compute(carry, key_block, value_block, step_block):
        run_max, run_sum, run_out = carry
        scores = (
            jnp.einsum("rhd,khd->hkr", q_heads, key_block, preferred_element_type=jnp.float32)
            * factor_scale
        )
        visible = step_block[None, :, None] <= q_steps[None, None, :]
        masked = jnp.where(visible, scores, LOW_SCORE)
        new_max = jnp.maximum(run_max, jnp.max(masked, axis=1))
        weights = jnp.where(visible, jnp.exp(masked - new_max[:, None, :]), 0.0)
        rescale = jnp.exp(run_max - new_max)
        new_sum = run_sum * rescale + jnp.sum(weights, axis=1)
        update = jnp.einsum(
            "hkr,khd->rhd",
            weights.astype(jnp.bfloat16),
            value_block,
            preferred_element_type=jnp.float32,
        )
        new_out = run_out * jnp.transpose(rescale)[:, :, None] + update
        return (new_max, new_sum, new_out)

    def visit(carry, block):
        key_block, value_block, step_block = block
        result = lax.cond(
            step_block[0] <= last_step,
            lambda state: compute(state, key_block, value_block, step_block),
            lambda state: state,
            carry,
        )
        return (result, None)

    initial = (
        jnp.full((head_count, row_count), LOW_SCORE, jnp.float32),
        jnp.zeros((head_count, row_count), jnp.float32),
        jnp.zeros((row_count, head_count, head_size), jnp.float32),
    )
    final_state, unused = lax.scan(visit, initial, blocks)
    return final_state


def on_device_blocks(queries, keys, values, step_of):
    block_rows, width = queries.shape
    head_size = HEAD_DIM
    head_count = width // head_size
    key_parts = lax.axis_size("ka")
    query_index = lax.axis_index("pb")
    key_index = lax.axis_index("ka")
    shard_rows = block_rows // key_parts
    half_rows = block_rows // 2
    key_count = keys.shape[0]
    first_steps = lax.dynamic_slice_in_dim(step_of, query_index * block_rows, half_rows)
    second_steps = lax.dynamic_slice_in_dim(
        step_of, query_index * block_rows + half_rows, half_rows
    )
    keys_mine, values_mine = (keys, values)
    key_steps = lax.dynamic_slice_in_dim(step_of, key_index * key_count, key_count)
    keys_all, values_all = (
        lax.all_gather(keys_mine, "pb", axis=1, tiled=True),
        lax.all_gather(values_mine, "pb", axis=1, tiled=True),
    )
    block_keys = math.gcd(64, key_count)
    first_state = attend_half(
        queries[:half_rows], first_steps, keys_all, values_all, key_steps, block_keys
    )
    second_state = attend_half(
        queries[half_rows:], second_steps, keys_all, values_all, key_steps, block_keys
    )
    row_max = jnp.concatenate([first_state[0], second_state[0]], axis=1)
    row_sum = jnp.concatenate([first_state[1], second_state[1]], axis=1)
    row_out = jnp.concatenate([first_state[2], second_state[2]], axis=0)
    sent = (
        jnp.transpose(row_max)[:, None, :],
        jnp.transpose(row_sum)[:, None, :],
        row_out.reshape(block_rows, 1, width),
    )
    got_max, got_sum, got_out = (
        lax.all_to_all(sent[0], "ka", split_axis=0, concat_axis=1, tiled=True),
        lax.all_to_all(sent[1], "ka", split_axis=0, concat_axis=1, tiled=True),
        lax.all_to_all(sent[2], "ka", split_axis=0, concat_axis=1, tiled=True),
    )
    best = jnp.max(got_max, axis=1, keepdims=True)
    weight = jnp.exp(got_max - best)
    total = jnp.sum(got_sum * weight, axis=1)
    shares = weight / total[:, None, :]
    pieces = got_out.reshape(shard_rows, key_parts, head_count, head_size) * shares[:, :, :, None]
    result = jnp.sum(pieces, axis=1).reshape(shard_rows, width)
    result = result.astype(jnp.bfloat16)
    return result


PARTS = 4
MESH = pl.DeviceIdType.MESH


def head_kernel(
    q_ref, k_ref, v_ref, step_ref, out_ref,
    qbuf, kbuf, vbuf, obuf, pbuf, held, held_lse, part_out, part_in, lse_out, lse_in, step_buf,
    q_send, k_send, v_send, o_send, part_send, lse_send,
    q_recv, k_recv, v_recv, o_recv, part_recv, lse_recv, step_sem,
    ready, entered_q, entered_k,
):
    head_size = HEAD_DIM
    parts_q = parts_k = PARTS
    p, a = lax.axis_index("pb"), lax.axis_index("ka")
    me = p * parts_k + a
    q_rows, k_rows = q_ref.shape[0], k_ref.shape[0]
    o_rows = out_ref.shape[0]
    seq = qbuf.shape[1]
    half = seq // 2
    block = 2 * o_rows
    factor = math.log2(math.e) / math.sqrt(head_size)
    barrier = pltpu.get_barrier_semaphore()

    def signal(sem, to_p, to_a):
        pl.semaphore_signal(
            sem, inc=1, device_id={"pb": to_p, "ka": to_a}, device_id_type=MESH
        )

    for other in range(1, parts_k):
        @pl.when(other > a)
        def _():
            signal(barrier, p, other)

    for other in range(1, parts_q):
        @pl.when(other > p)
        def _():
            signal(barrier, other, a)

    @pl.when(a + p > 0)
    def _():
        pl.semaphore_wait(barrier, a + p)

    for other in range(parts_k - 1):
        @pl.when(other < a)
        def _():
            signal(entered_k.at[a], p, other)

    for other in range(parts_q - 1):
        @pl.when(other < p)
        def _():
            signal(entered_q.at[p], other, a)

    def head_columns(index):
        return pl.ds(pl.multiple_of(index * head_size, head_size), head_size)

    q_place = pl.ds(pl.multiple_of(p * q_rows, q_rows), q_rows)

    def keys_of(layer, local, slot):
        place = slice(layer * k_rows, (layer + 1) * k_rows)
        column = slice(local * head_size, (local + 1) * head_size)
        for source, target, sem in ((k_ref, kbuf, k_recv), (v_ref, vbuf, v_recv)):
            pltpu.make_async_copy(
                source.at[:, column], target.at[slot, place], sem.at[slot, layer]
            ).start()

    def send_keys(layer, local, slot, to, rows=None):
        rows = k_rows if rows is None else rows
        place = slice(layer * k_rows, layer * k_rows + rows)
        column = slice(local * head_size, (local + 1) * head_size)
        for source, target, sent, sem in (
            (k_ref, kbuf, k_send, k_recv), (v_ref, vbuf, v_send, v_recv)
        ):
            pltpu.make_async_remote_copy(
                src_ref=source.at[:rows, column], dst_ref=target.at[slot, place],
                send_sem=sent.at[local], recv_sem=sem.at[slot, layer],
                device_id={"pb": p, "ka": to}, device_id_type=MESH,
            ).start()

    def wait_keys_sent(local, rows):
        for source, sent in ((kbuf, k_send), (vbuf, v_send)):
            piece = source.at[0, :rows]
            pltpu.make_async_copy(piece, piece, sent.at[local]).wait()

    @pl.when(a == 0)
    def _():
        keys_of(0, 0, 0)
        pl.semaphore_wait(entered_k.at[1], 1)
        send_keys(0, 1, 0, 1)
        pl.semaphore_wait(entered_k.at[3], 1)
        send_keys(0, 3, 0, 3)
        send_keys(0, 2, 1, 1)
        pl.semaphore_wait(entered_k.at[2], 1)

    @pl.when(a == 1)
    def _():
        keys_of(1, 1, 0)
        keys_of(1, 2, 1)
        send_keys(1, 0, 0, 0)
        pl.semaphore_wait(entered_k.at[3], 1)
        send_keys(1, 3, 0, 3)
        pl.semaphore_wait(entered_k.at[2], 1)

    @pl.when(a == 2)
    def _():
        keys_of(2, 1, 0)
        keys_of(2, 2, 1)
        send_keys(2, 0, 0, 0)
        send_keys(2, 1, 0, 1, o_rows)
        pl.semaphore_wait(entered_k.at[3], 1)
        send_keys(2, 3, 0, 3)
        send_keys(2, 2, 1, 1, o_rows)

    @pl.when(a == 3)
    def _():
        keys_of(3, 3, 0)
        send_keys(3, 1, 0, 2)
        send_keys(3, 0, 0, 0)
        send_keys(3, 2, 1, 2)

    step_copy = pltpu.make_async_copy(step_ref, step_buf, step_sem)
    step_copy.start()

    split = jnp.logical_or(a == 1, a == 2)
    sends_q = jnp.logical_or(a != 2, p >= parts_q // 2)

    for to in reversed(range(parts_q)):
        @pl.when(p != to)
        def _():
            @pl.when(to > p)
            def _():
                pl.semaphore_wait(entered_q.at[to], 1)

            signal(ready.at[p], to, a)

    def send_queries(slot, local):
        for to in reversed(range(parts_q)):
            source = q_ref.at[:, head_columns(to * parts_k + local)]

            @pl.when(p != to)
            def _():
                pltpu.make_async_remote_copy(
                    src_ref=source, dst_ref=qbuf.at[slot, q_place],
                    send_sem=q_send.at[slot, to], recv_sem=q_recv.at[slot, p],
                    device_id={"pb": to, "ka": a}, device_id_type=MESH,
                ).start()

            @pl.when(p == to)
            def _():
                pltpu.make_async_copy(
                    source, qbuf.at[slot, q_place], q_recv.at[slot, p]
                ).start()

    @pl.when(sends_q)
    def _():
        send_queries(0, jnp.where(split, 1, a))

    @pl.when(jnp.logical_and(sends_q, split))
    def _():
        send_queries(1, 2)

    step_copy.wait()
    steps = step_buf[...].astype(jnp.float32)
    for other in range(parts_q):
        @pl.when(p != other)
        def _():
            pl.semaphore_wait(ready.at[other], 1)

    def arrived(piece, sem):
        pltpu.make_async_copy(piece, piece, sem).wait()

    def queries_in(slot, part):
        arrived(qbuf.at[slot, part * q_rows:(part + 1) * q_rows], q_recv.at[slot, part])

    def keys_in(slot, layer, rows=None):
        rows = k_rows if rows is None else rows
        place = slice(layer * k_rows, layer * k_rows + rows)
        arrived(kbuf.at[slot, place], k_recv.at[slot, layer])
        arrived(vbuf.at[slot, place], v_recv.at[slot, layer])

    def attend(slot, start, low, middle, high):
        stop = start + block
        q_block = qbuf[slot, start:stop, :]
        pieces = [(one, two) for one, two in ((low, middle), (middle, high)) if two > one]
        scores = []
        for one, two in pieces:
            score = lax.dot_general(
                q_block, kbuf[slot, one:two, :], (((1,), (1,)), ((), ())),
                preferred_element_type=jnp.float32,
            )
            if one >= middle:
                q_steps = jnp.concatenate(
                    [
                        jnp.transpose(jnp.broadcast_to(steps[:, row:row + 128], (128, 128)))
                        for row in range(start, stop, 128)
                    ],
                    axis=0,
                )
                visible = jnp.concatenate(
                    [steps[:, row:row + 128] <= q_steps for row in range(one, two, 128)],
                    axis=1,
                )
                score = jnp.where(visible, score, LOW_SCORE)
            scores.append(score)
        row_max = jnp.max(scores[0], axis=1, keepdims=True)
        for score in scores[1:]:
            row_max = jnp.maximum(row_max, jnp.max(score, axis=1, keepdims=True))
        total = None
        for (one, two), score in zip(pieces, scores):
            weights = jnp.exp2((score - row_max) * factor)
            part = jnp.sum(weights, axis=1, keepdims=True)
            pbuf[start:stop, one:two] = weights.astype(jnp.bfloat16)
            total = part if total is None else total + part
        mixed = jnp.dot(
            pbuf[start:stop, low:high], vbuf[slot, low:high, :],
            preferred_element_type=jnp.float32,
        )
        return mixed / total, row_max * factor + jnp.log2(total)

    def deliver(slot, head, start, result):
        obuf[slot, start:start + block, :] = result.astype(jnp.bfloat16)
        for shard in range(start // o_rows, (start + block) // o_rows):
            source = obuf.at[slot, shard * o_rows:(shard + 1) * o_rows]
            target = out_ref.at[:, head_columns(head)]

            @pl.when(me == shard)
            def _():
                pltpu.make_async_copy(source, target, o_recv.at[head]).start()

            @pl.when(me != shard)
            def _():
                pltpu.make_async_remote_copy(
                    src_ref=source, dst_ref=target,
                    send_sem=o_send.at[slot, shard], recv_sem=o_recv.at[head],
                    device_id={"pb": shard // parts_k, "ka": shard % parts_k},
                    device_id_type=MESH,
                ).start()

    def delivered(slot, starts):
        for start in starts:
            for shard in range(start // o_rows, (start + block) // o_rows):
                @pl.when(me != shard)
                def _():
                    arrived(
                        obuf.at[slot, shard * o_rows:(shard + 1) * o_rows],
                        o_send.at[slot, shard],
                    )

    def part_copies(slot, index, to):
        return [
            pltpu.make_async_remote_copy(
                src_ref=source.at[slot, index], dst_ref=target.at[slot, index],
                send_sem=sent.at[slot, index], recv_sem=sem.at[slot, index],
                device_id={"pb": p, "ka": to}, device_id_type=MESH,
            )
            for source, target, sent, sem in (
                (part_out, part_in, part_send, part_recv), (lse_out, lse_in, lse_send, lse_recv)
            )
        ]

    def pass_on(slot, index, to, result, lse):
        part_out[slot, index] = result.astype(jnp.bfloat16)
        for i in range(block // 128):
            row = jnp.transpose(jnp.broadcast_to(lse[i * 128:(i + 1) * 128], (128, 128)))
            lse_out[slot, index, i * 8:(i + 1) * 8, :] = row[:8]
        for copy in part_copies(slot, index, to):
            copy.start()

    def hold(slot, index, result, lse):
        held[slot, index] = result
        held_lse[slot, index] = jnp.broadcast_to(lse, (block, 128))

    def merged(slot, index, to):
        for copy in part_copies(slot, index, to):
            copy.wait_recv()
        other_lse = jnp.concatenate(
            [
                jnp.transpose(
                    jnp.broadcast_to(lse_in[slot, index, i * 8:i * 8 + 1, :], (128, 128))
                )
                for i in range(block // 128)
            ],
            axis=0,
        )
        mine_lse = held_lse[slot, index]
        best = jnp.maximum(mine_lse, other_lse)
        mine, other = jnp.exp2(mine_lse - best), jnp.exp2(other_lse - best)
        both = held[slot, index] * mine + part_in[slot, index].astype(jnp.float32) * other
        return both / (mine + other)

    low_side = [half, half + 2 * block]
    high_side = [half + block, half + 3 * block]

    @pl.when(jnp.logical_not(split))
    def _():
        have_q = have_k = 0
        for start in range(0, seq, block):
            stop = start + block
            high = min(stop + 128, seq)
            while have_q * q_rows < stop:
                queries_in(0, have_q)
                have_q += 1
            while have_k * k_rows < high:
                keys_in(0, have_k)
                have_k += 1
            result, unused = attend(0, start, 0, start, high)
            deliver(0, p * parts_k + a, start, result)
        delivered(0, range(0, seq, block))

    @pl.when(a == 1)
    def _():
        def one_head(slot, carry):
            head = p * parts_k + 1 + slot
            keys_in(slot, 1)
            for part in (2, 3):
                queries_in(slot, part)
            keys_in(slot, 0)
            for index, start in enumerate(high_side):
                pass_on(slot, index, 2, *attend(slot, start, 0, half, half))
            for part in (0, 1):
                queries_in(slot, part)
            keys_in(slot, 2, o_rows)
            for start in (3 * block, block, 2 * block, 0):
                result, unused = attend(slot, start, 0, start, start + block + 128)
                deliver(slot, head, start, result)
            for index, start in enumerate(low_side):
                hold(slot, index, *attend(slot, start, 0, half, half))
            for index, start in enumerate(low_side):
                deliver(slot, head, start, merged(slot, index, 2))
            return carry

        lax.fori_loop(0, 2, one_head, 0)
        for slot in range(2):
            for index in range(2):
                for copy in part_copies(slot, index, 2):
                    copy.wait_send()
            delivered(slot, [*range(0, half, block), *low_side])

    @pl.when(a == 2)
    def _():
        def one_head(slot, carry):
            keys_in(slot, 2)
            queries_in(slot, 2)
            queries_in(slot, 3)
            keys_in(slot, 3)
            for index, start in enumerate(low_side):
                pass_on(slot, index, 1, *attend(slot, start, half, start, start + block + 128))
            for index, start in enumerate(high_side):
                high = min(start + block + 128, seq)
                hold(slot, index, *attend(slot, start, half, start, high))
            return carry

        def merge_head(slot, carry):
            head = p * parts_k + 1 + slot
            for index, start in enumerate(high_side):
                deliver(slot, head, start, merged(slot, index, 1))
            return carry

        lax.fori_loop(0, 2, one_head, 0)
        lax.fori_loop(0, 2, merge_head, 0)
        for slot in range(2):
            for index in range(2):
                for copy in part_copies(slot, index, 1):
                    copy.wait_send()
            delivered(slot, high_side)

    for layer, sent in enumerate((
        ((1, k_rows), (3, k_rows), (2, k_rows)),
        ((3, k_rows), (0, k_rows)),
        ((0, k_rows), (1, o_rows), (3, k_rows), (2, o_rows)),
        ((1, k_rows), (0, k_rows), (2, k_rows)),
    )):
        @pl.when(a == layer)
        def _():
            for local, rows in sent:
                wait_keys_sent(local, rows)

    def wait_queries_sent(slot):
        for to in range(parts_q):
            @pl.when(p != to)
            def _():
                arrived(qbuf.at[slot, :q_rows], q_send.at[slot, to])

    @pl.when(sends_q)
    def _():
        wait_queries_sent(0)

    @pl.when(jnp.logical_and(sends_q, split))
    def _():
        wait_queries_sent(1)

    for head in range(parts_q * parts_k):
        arrived(out_ref.at[:, head * head_size:(head + 1) * head_size], o_recv.at[head])


def on_device_heads(queries, keys, values, step_of):
    block_rows, width = queries.shape
    seq = step_of.shape[0]
    shard_rows = block_rows // PARTS
    block = 2 * shard_rows
    buffer = pltpu.VMEM((2, seq, HEAD_DIM), jnp.bfloat16)
    anywhere = pl.BlockSpec(memory_space=pltpu.HBM)
    dma = pltpu.SemaphoreType.DMA
    return pl.pallas_call(
        head_kernel,
        out_shape=jax.ShapeDtypeStruct((shard_rows, width), jnp.bfloat16),
        in_specs=[anywhere, anywhere, anywhere, anywhere],
        out_specs=pl.BlockSpec(memory_space=pltpu.VMEM),
        scratch_shapes=[
            buffer, buffer, buffer, buffer,
            pltpu.VMEM((seq, seq), jnp.bfloat16),
            pltpu.VMEM((2, 2, block, HEAD_DIM), jnp.float32),
            pltpu.VMEM((2, 2, block, HEAD_DIM), jnp.float32),
            pltpu.VMEM((2, 2, block, HEAD_DIM), jnp.bfloat16),
            pltpu.VMEM((2, 2, block, HEAD_DIM), jnp.bfloat16),
            pltpu.VMEM((2, 2, block // 16, 128), jnp.float32),
            pltpu.VMEM((2, 2, block // 16, 128), jnp.float32),
            pltpu.VMEM((1, seq), jnp.int32),
            dma((2, PARTS)), dma((PARTS,)), dma((PARTS,)), dma((2, PARTS * PARTS)),
            dma((2, 2)), dma((2, 2)),
            dma((2, PARTS)), dma((2, PARTS)), dma((2, PARTS)), dma((PARTS * PARTS,)),
            dma((2, 2)), dma((2, 2)), dma,
            pltpu.SemaphoreType.REGULAR((PARTS,)),
            pltpu.SemaphoreType.REGULAR((PARTS,)),
            pltpu.SemaphoreType.REGULAR((PARTS,)),
        ],
        compiler_params=pltpu.CompilerParams(
            collective_id=0, has_side_effects=True, vmem_limit_bytes=48 * 1024 * 1024
        ),
    )(*[
        pltpu.with_memory_space_constraint(array, pltpu.HBM)
        for array in (queries, keys, values, step_of.reshape(1, seq))
    ])


def head_per_device(mesh_shape, queries, keys, step_of):
    return (
        mesh_shape["pb"] == PARTS
        and mesh_shape["ka"] == PARTS
        and keys.shape[1] == PARTS * HEAD_DIM
        and step_of.shape[0] == PARTS * PARTS * 128
    )


def solution(mesh):
    placed = (
        P(("groups", "pb"), None),
        P(("groups", "ka"), "pb"),
        P(("groups", "ka"), "pb"),
        P("groups"),
    )

    def on_device(queries, keys, values, step_of):
        if head_per_device(mesh.shape, queries, keys, step_of):
            return on_device_heads(queries, keys, values, step_of)
        return on_device_blocks(queries, keys, values, step_of)

    return jax.shard_map(
        on_device,
        mesh=mesh,
        in_specs=placed,
        out_specs=P(("groups", "pb", "ka"), None),
        check_vma=False,
    )
```

```python
import functools
import math

import jax
import jax.numpy as jnp
from jax import lax
from jax.experimental import pallas as pl
from jax.experimental.pallas import tpu as pltpu
from jax.sharding import PartitionSpec as P

HEAD_DIM = 128


LOW_SCORE = -1e30


def attend_half(q_rows, q_steps, keys_all, values_all, key_steps, block_keys):
    row_count, width = q_rows.shape
    head_size = HEAD_DIM
    head_count = width // head_size
    key_count = keys_all.shape[0]
    block_count = key_count // block_keys
    factor_scale = 1.0 / math.sqrt(head_size)
    q_heads = q_rows.reshape(row_count, head_count, head_size)
    blocks = (
        keys_all.reshape(block_count, block_keys, head_count, head_size),
        values_all.reshape(block_count, block_keys, head_count, head_size),
        key_steps.reshape(block_count, block_keys),
    )
    last_step = q_steps[row_count - 1]

    def compute(carry, key_block, value_block, step_block):
        run_max, run_sum, run_out = carry
        scores = (
            jnp.einsum("rhd,khd->hkr", q_heads, key_block, preferred_element_type=jnp.float32)
            * factor_scale
        )
        visible = step_block[None, :, None] <= q_steps[None, None, :]
        masked = jnp.where(visible, scores, LOW_SCORE)
        new_max = jnp.maximum(run_max, jnp.max(masked, axis=1))
        weights = jnp.where(visible, jnp.exp(masked - new_max[:, None, :]), 0.0)
        rescale = jnp.exp(run_max - new_max)
        new_sum = run_sum * rescale + jnp.sum(weights, axis=1)
        update = jnp.einsum(
            "hkr,khd->rhd",
            weights.astype(jnp.bfloat16),
            value_block,
            preferred_element_type=jnp.float32,
        )
        new_out = run_out * jnp.transpose(rescale)[:, :, None] + update
        return (new_max, new_sum, new_out)

    def visit(carry, block):
        key_block, value_block, step_block = block
        result = lax.cond(
            step_block[0] <= last_step,
            lambda state: compute(state, key_block, value_block, step_block),
            lambda state: state,
            carry,
        )
        return (result, None)

    initial = (
        jnp.full((head_count, row_count), LOW_SCORE, jnp.float32),
        jnp.zeros((head_count, row_count), jnp.float32),
        jnp.zeros((row_count, head_count, head_size), jnp.float32),
    )
    final_state, unused = lax.scan(visit, initial, blocks)
    return final_state


def on_device_blocks(queries, keys, values, step_of):
    block_rows, width = queries.shape
    head_size = HEAD_DIM
    head_count = width // head_size
    key_parts = lax.axis_size("ka")
    query_index = lax.axis_index("pb")
    key_index = lax.axis_index("ka")
    shard_rows = block_rows // key_parts
    half_rows = block_rows // 2
    key_count = keys.shape[0]
    first_steps = lax.dynamic_slice_in_dim(step_of, query_index * block_rows, half_rows)
    second_steps = lax.dynamic_slice_in_dim(
        step_of, query_index * block_rows + half_rows, half_rows
    )
    keys_mine, values_mine = (keys, values)
    key_steps = lax.dynamic_slice_in_dim(step_of, key_index * key_count, key_count)
    keys_all, values_all = (
        lax.all_gather(keys_mine, "pb", axis=1, tiled=True),
        lax.all_gather(values_mine, "pb", axis=1, tiled=True),
    )
    block_keys = math.gcd(64, key_count)
    first_state = attend_half(
        queries[:half_rows], first_steps, keys_all, values_all, key_steps, block_keys
    )
    second_state = attend_half(
        queries[half_rows:], second_steps, keys_all, values_all, key_steps, block_keys
    )
    row_max = jnp.concatenate([first_state[0], second_state[0]], axis=1)
    row_sum = jnp.concatenate([first_state[1], second_state[1]], axis=1)
    row_out = jnp.concatenate([first_state[2], second_state[2]], axis=0)
    sent = (
        jnp.transpose(row_max)[:, None, :],
        jnp.transpose(row_sum)[:, None, :],
        row_out.reshape(block_rows, 1, width),
    )
    got_max, got_sum, got_out = (
        lax.all_to_all(sent[0], "ka", split_axis=0, concat_axis=1, tiled=True),
        lax.all_to_all(sent[1], "ka", split_axis=0, concat_axis=1, tiled=True),
        lax.all_to_all(sent[2], "ka", split_axis=0, concat_axis=1, tiled=True),
    )
    best = jnp.max(got_max, axis=1, keepdims=True)
    weight = jnp.exp(got_max - best)
    total = jnp.sum(got_sum * weight, axis=1)
    shares = weight / total[:, None, :]
    pieces = got_out.reshape(shard_rows, key_parts, head_count, head_size) * shares[:, :, :, None]
    result = jnp.sum(pieces, axis=1).reshape(shard_rows, width)
    result = result.astype(jnp.bfloat16)
    return result


PARTS = 4
MESH = pl.DeviceIdType.MESH


def head_kernel(
    q_ref, k_ref, v_ref, step_ref, out_ref,
    qbuf, kbuf, vbuf, obuf, pbuf, held, held_lse, part_out, part_in, lse_out, lse_in, step_buf,
    q_send, k_send, v_send, o_send, part_send, lse_send,
    q_recv, k_recv, v_recv, o_recv, part_recv, lse_recv, step_sem,
    ready, entered_q, entered_k,
):
    head_size = HEAD_DIM
    parts_q = parts_k = PARTS
    p, a = lax.axis_index("pb"), lax.axis_index("ka")
    me = p * parts_k + a
    q_rows, k_rows = q_ref.shape[0], k_ref.shape[0]
    o_rows = out_ref.shape[0]
    seq = qbuf.shape[1]
    half = seq // 2
    block = 2 * o_rows
    factor = math.log2(math.e) / math.sqrt(head_size)
    barrier = pltpu.get_barrier_semaphore()

    def signal(sem, to_p, to_a):
        pl.semaphore_signal(
            sem, inc=1, device_id={"pb": to_p, "ka": to_a}, device_id_type=MESH
        )

    for other in range(1, parts_k):
        @pl.when(other > a)
        def _():
            signal(barrier, p, other)

    for other in range(1, parts_q):
        @pl.when(other > p)
        def _():
            signal(barrier, other, a)

    @pl.when(a + p > 0)
    def _():
        pl.semaphore_wait(barrier, a + p)

    for other in range(parts_k - 1):
        @pl.when(other < a)
        def _():
            signal(entered_k.at[a], p, other)

    for other in range(parts_q - 1):
        @pl.when(other < p)
        def _():
            signal(entered_q.at[p], other, a)

    def head_columns(index):
        return pl.ds(pl.multiple_of(index * head_size, head_size), head_size)

    q_place = pl.ds(pl.multiple_of(p * q_rows, q_rows), q_rows)

    def keys_of(layer, local, slot):
        place = slice(layer * k_rows, (layer + 1) * k_rows)
        column = slice(local * head_size, (local + 1) * head_size)
        for source, target, sem in ((k_ref, kbuf, k_recv), (v_ref, vbuf, v_recv)):
            pltpu.make_async_copy(
                source.at[:, column], target.at[slot, place], sem.at[slot, layer]
            ).start()

    def send_keys(layer, local, slot, to, rows=None):
        rows = k_rows if rows is None else rows
        place = slice(layer * k_rows, layer * k_rows + rows)
        column = slice(local * head_size, (local + 1) * head_size)
        for source, target, sent, sem in (
            (k_ref, kbuf, k_send, k_recv), (v_ref, vbuf, v_send, v_recv)
        ):
            pltpu.make_async_remote_copy(
                src_ref=source.at[:rows, column], dst_ref=target.at[slot, place],
                send_sem=sent.at[local], recv_sem=sem.at[slot, layer],
                device_id={"pb": p, "ka": to}, device_id_type=MESH,
            ).start()

    def wait_keys_sent(local, rows):
        for source, sent in ((kbuf, k_send), (vbuf, v_send)):
            piece = source.at[0, :rows]
            pltpu.make_async_copy(piece, piece, sent.at[local]).wait()

    @pl.when(a == 0)
    def _():
        keys_of(0, 0, 0)
        pl.semaphore_wait(entered_k.at[1], 1)
        send_keys(0, 1, 0, 1)
        pl.semaphore_wait(entered_k.at[3], 1)
        send_keys(0, 3, 0, 3)
        send_keys(0, 2, 1, 1)
        pl.semaphore_wait(entered_k.at[2], 1)

    @pl.when(a == 1)
    def _():
        keys_of(1, 1, 0)
        keys_of(1, 2, 1)
        send_keys(1, 0, 0, 0)
        pl.semaphore_wait(entered_k.at[3], 1)
        send_keys(1, 3, 0, 3)
        pl.semaphore_wait(entered_k.at[2], 1)

    @pl.when(a == 2)
    def _():
        keys_of(2, 1, 0)
        keys_of(2, 2, 1)
        send_keys(2, 0, 0, 0)
        send_keys(2, 1, 0, 1, o_rows)
        pl.semaphore_wait(entered_k.at[3], 1)
        send_keys(2, 3, 0, 3)
        send_keys(2, 2, 1, 1, o_rows)

    @pl.when(a == 3)
    def _():
        keys_of(3, 3, 0)
        send_keys(3, 1, 0, 2)
        send_keys(3, 0, 0, 0)
        send_keys(3, 2, 1, 2)

    step_copy = pltpu.make_async_copy(step_ref, step_buf, step_sem)
    step_copy.start()

    split = jnp.logical_or(a == 1, a == 2)
    sends_q = jnp.logical_or(a != 2, p >= parts_q // 2)

    for to in reversed(range(parts_q)):
        @pl.when(p != to)
        def _():
            @pl.when(to > p)
            def _():
                pl.semaphore_wait(entered_q.at[to], 1)

            signal(ready.at[p], to, a)

    def send_queries(slot, local):
        for to in reversed(range(parts_q)):
            source = q_ref.at[:, head_columns(to * parts_k + local)]

            @pl.when(p != to)
            def _():
                pltpu.make_async_remote_copy(
                    src_ref=source, dst_ref=qbuf.at[slot, q_place],
                    send_sem=q_send.at[slot, to], recv_sem=q_recv.at[slot, p],
                    device_id={"pb": to, "ka": a}, device_id_type=MESH,
                ).start()

            @pl.when(p == to)
            def _():
                pltpu.make_async_copy(
                    source, qbuf.at[slot, q_place], q_recv.at[slot, p]
                ).start()

    @pl.when(sends_q)
    def _():
        send_queries(0, jnp.where(split, 1, a))

    @pl.when(jnp.logical_and(sends_q, split))
    def _():
        send_queries(1, 2)

    step_copy.wait()
    steps = step_buf[...].astype(jnp.float32)
    for other in range(parts_q):
        @pl.when(p != other)
        def _():
            pl.semaphore_wait(ready.at[other], 1)

    def arrived(piece, sem):
        pltpu.make_async_copy(piece, piece, sem).wait()

    def queries_in(slot, part):
        arrived(qbuf.at[slot, part * q_rows:(part + 1) * q_rows], q_recv.at[slot, part])

    def keys_in(slot, layer, rows=None):
        rows = k_rows if rows is None else rows
        place = slice(layer * k_rows, layer * k_rows + rows)
        arrived(kbuf.at[slot, place], k_recv.at[slot, layer])
        arrived(vbuf.at[slot, place], v_recv.at[slot, layer])

    def attend(slot, start, low, middle, high):
        stop = start + block
        q_block = qbuf[slot, start:stop, :]
        pieces = [(one, two) for one, two in ((low, middle), (middle, high)) if two > one]
        scores = []
        for one, two in pieces:
            score = lax.dot_general(
                q_block, kbuf[slot, one:two, :], (((1,), (1,)), ((), ())),
                preferred_element_type=jnp.float32,
            )
            if one >= middle:
                q_steps = jnp.concatenate(
                    [
                        jnp.transpose(jnp.broadcast_to(steps[:, row:row + 128], (128, 128)))
                        for row in range(start, stop, 128)
                    ],
                    axis=0,
                )
                visible = jnp.concatenate(
                    [steps[:, row:row + 128] <= q_steps for row in range(one, two, 128)],
                    axis=1,
                )
                score = jnp.where(visible, score, LOW_SCORE)
            scores.append(score)
        row_max = jnp.max(scores[0], axis=1, keepdims=True)
        for score in scores[1:]:
            row_max = jnp.maximum(row_max, jnp.max(score, axis=1, keepdims=True))
        total = None
        for (one, two), score in zip(pieces, scores):
            weights = jnp.exp2((score - row_max) * factor)
            part = jnp.sum(weights, axis=1, keepdims=True)
            pbuf[start:stop, one:two] = weights.astype(jnp.bfloat16)
            total = part if total is None else total + part
        mixed = jnp.dot(
            pbuf[start:stop, low:high], vbuf[slot, low:high, :],
            preferred_element_type=jnp.float32,
        )
        return mixed / total, row_max * factor + jnp.log2(total)

    def deliver(slot, head, start, result):
        obuf[slot, start:start + block, :] = result.astype(jnp.bfloat16)
        for shard in range(start // o_rows, (start + block) // o_rows):
            source = obuf.at[slot, shard * o_rows:(shard + 1) * o_rows]
            target = out_ref.at[:, head_columns(head)]

            @pl.when(me == shard)
            def _():
                pltpu.make_async_copy(source, target, o_recv.at[head]).start()

            @pl.when(me != shard)
            def _():
                pltpu.make_async_remote_copy(
                    src_ref=source, dst_ref=target,
                    send_sem=o_send.at[slot, shard], recv_sem=o_recv.at[head],
                    device_id={"pb": shard // parts_k, "ka": shard % parts_k},
                    device_id_type=MESH,
                ).start()

    def delivered(slot, starts):
        for start in starts:
            for shard in range(start // o_rows, (start + block) // o_rows):
                @pl.when(me != shard)
                def _():
                    arrived(
                        obuf.at[slot, shard * o_rows:(shard + 1) * o_rows],
                        o_send.at[slot, shard],
                    )

    def part_copies(slot, index, to):
        return [
            pltpu.make_async_remote_copy(
                src_ref=source.at[slot, index], dst_ref=target.at[slot, index],
                send_sem=sent.at[slot, index], recv_sem=sem.at[slot, index],
                device_id={"pb": p, "ka": to}, device_id_type=MESH,
            )
            for source, target, sent, sem in (
                (part_out, part_in, part_send, part_recv), (lse_out, lse_in, lse_send, lse_recv)
            )
        ]

    def pass_on(slot, index, to, result, lse):
        part_out[slot, index] = result.astype(jnp.bfloat16)
        for i in range(block // 128):
            row = jnp.transpose(jnp.broadcast_to(lse[i * 128:(i + 1) * 128], (128, 128)))
            lse_out[slot, index, i:i + 1, :] = row[:1]
        for copy in part_copies(slot, index, to):
            copy.start()

    def hold(slot, index, result, lse):
        held[slot, index] = result
        held_lse[slot, index] = jnp.broadcast_to(lse, (block, 128))

    def merged(slot, index, to):
        for copy in part_copies(slot, index, to):
            copy.wait_recv()
        other_lse = jnp.concatenate(
            [
                jnp.transpose(
                    jnp.broadcast_to(lse_in[slot, index, i:i + 1, :], (128, 128))
                )
                for i in range(block // 128)
            ],
            axis=0,
        )
        mine_lse = held_lse[slot, index]
        best = jnp.maximum(mine_lse, other_lse)
        mine, other = jnp.exp2(mine_lse - best), jnp.exp2(other_lse - best)
        both = held[slot, index] * mine + part_in[slot, index].astype(jnp.float32) * other
        return both / (mine + other)

    low_side = [half, half + 2 * block]
    high_side = [half + block, half + 3 * block]

    @pl.when(jnp.logical_not(split))
    def _():
        have_q = have_k = 0
        for start in range(0, seq, block):
            stop = start + block
            high = min(stop + 128, seq)
            while have_q * q_rows < stop:
                queries_in(0, have_q)
                have_q += 1
            while have_k * k_rows < high:
                keys_in(0, have_k)
                have_k += 1
            result, unused = attend(0, start, 0, start, high)
            deliver(0, p * parts_k + a, start, result)
        delivered(0, range(0, seq, block))

    @pl.when(a == 1)
    def _():
        def one_head(slot, carry):
            head = p * parts_k + 1 + slot
            keys_in(slot, 1)
            for part in (2, 3):
                queries_in(slot, part)
            keys_in(slot, 0)
            for index, start in enumerate(high_side):
                pass_on(slot, index, 2, *attend(slot, start, 0, half, half))
            for part in (0, 1):
                queries_in(slot, part)
            keys_in(slot, 2, o_rows)
            for start in (3 * block, block, 2 * block, 0):
                result, unused = attend(slot, start, 0, start, start + block + 128)
                deliver(slot, head, start, result)
            for index, start in enumerate(low_side):
                hold(slot, index, *attend(slot, start, 0, half, half))
            return carry

        def merge_head(slot, carry):
            head = p * parts_k + 1 + slot
            for index, start in enumerate(low_side):
                deliver(slot, head, start, merged(slot, index, 2))
            return carry

        def next_head(slot, carry):
            one_head(slot, carry)

            @pl.when(slot > 0)
            def _():
                merge_head(slot - 1, carry)

            return carry

        lax.fori_loop(0, 2, next_head, 0)
        merge_head(2 - 1, 0)
        for slot in range(2):
            for index in range(2):
                for copy in part_copies(slot, index, 2):
                    copy.wait_send()
            delivered(slot, [*range(0, half, block), *low_side])

    @pl.when(a == 2)
    def _():
        def one_head(slot, carry):
            keys_in(slot, 2)
            queries_in(slot, 2)
            queries_in(slot, 3)
            keys_in(slot, 3)
            for index, start in enumerate(low_side):
                pass_on(slot, index, 1, *attend(slot, start, half, start, start + block + 128))
            for index, start in enumerate(high_side):
                high = min(start + block + 128, seq)
                hold(slot, index, *attend(slot, start, half, start, high))
            return carry

        def merge_head(slot, carry):
            head = p * parts_k + 1 + slot
            for index, start in enumerate(high_side):
                deliver(slot, head, start, merged(slot, index, 1))
            return carry

        lax.fori_loop(0, 2, one_head, 0)
        lax.fori_loop(0, 2, merge_head, 0)
        for slot in range(2):
            for index in range(2):
                for copy in part_copies(slot, index, 1):
                    copy.wait_send()
            delivered(slot, high_side)

    for layer, sent in enumerate((
        ((1, k_rows), (3, k_rows), (2, k_rows)),
        ((3, k_rows), (0, k_rows)),
        ((0, k_rows), (1, o_rows), (3, k_rows), (2, o_rows)),
        ((1, k_rows), (0, k_rows), (2, k_rows)),
    )):
        @pl.when(a == layer)
        def _():
            for local, rows in sent:
                wait_keys_sent(local, rows)

    def wait_queries_sent(slot):
        for to in range(parts_q):
            @pl.when(p != to)
            def _():
                arrived(qbuf.at[slot, :q_rows], q_send.at[slot, to])

    @pl.when(sends_q)
    def _():
        wait_queries_sent(0)

    @pl.when(jnp.logical_and(sends_q, split))
    def _():
        wait_queries_sent(1)

    for head in range(parts_q * parts_k):
        arrived(out_ref.at[:, head * head_size:(head + 1) * head_size], o_recv.at[head])


def on_device_heads(queries, keys, values, step_of):
    block_rows, width = queries.shape
    seq = step_of.shape[0]
    shard_rows = block_rows // PARTS
    block = 2 * shard_rows
    buffer = pltpu.VMEM((2, seq, HEAD_DIM), jnp.bfloat16)
    anywhere = pl.BlockSpec(memory_space=pltpu.HBM)
    dma = pltpu.SemaphoreType.DMA
    return pl.pallas_call(
        head_kernel,
        out_shape=jax.ShapeDtypeStruct((shard_rows, width), jnp.bfloat16),
        in_specs=[anywhere, anywhere, anywhere, anywhere],
        out_specs=pl.BlockSpec(memory_space=pltpu.VMEM),
        scratch_shapes=[
            buffer, buffer, buffer, buffer,
            pltpu.VMEM((seq, seq), jnp.bfloat16),
            pltpu.VMEM((2, 2, block, HEAD_DIM), jnp.float32),
            pltpu.VMEM((2, 2, block, HEAD_DIM), jnp.float32),
            pltpu.VMEM((2, 2, block, HEAD_DIM), jnp.bfloat16),
            pltpu.VMEM((2, 2, block, HEAD_DIM), jnp.bfloat16),
            pltpu.VMEM((2, 2, 8, 128), jnp.float32),
            pltpu.VMEM((2, 2, 8, 128), jnp.float32),
            pltpu.VMEM((1, seq), jnp.int32),
            dma((2, PARTS)), dma((PARTS,)), dma((PARTS,)), dma((2, PARTS * PARTS)),
            dma((2, 2)), dma((2, 2)),
            dma((2, PARTS)), dma((2, PARTS)), dma((2, PARTS)), dma((PARTS * PARTS,)),
            dma((2, 2)), dma((2, 2)), dma,
            pltpu.SemaphoreType.REGULAR((PARTS,)),
            pltpu.SemaphoreType.REGULAR((PARTS,)),
            pltpu.SemaphoreType.REGULAR((PARTS,)),
        ],
        compiler_params=pltpu.CompilerParams(
            collective_id=0, has_side_effects=True, vmem_limit_bytes=48 * 1024 * 1024
        ),
    )(*[
        pltpu.with_memory_space_constraint(array, pltpu.HBM)
        for array in (queries, keys, values, step_of.reshape(1, seq))
    ])


def head_per_device(mesh_shape, queries, keys, step_of):
    return (
        mesh_shape["pb"] == PARTS
        and mesh_shape["ka"] == PARTS
        and keys.shape[1] == PARTS * HEAD_DIM
        and step_of.shape[0] == PARTS * PARTS * 128
    )


def solution(mesh):
    placed = (
        P(("groups", "pb"), None),
        P(("groups", "ka"), "pb"),
        P(("groups", "ka"), "pb"),
        P("groups"),
    )

    def on_device(queries, keys, values, step_of):
        if head_per_device(mesh.shape, queries, keys, step_of):
            return on_device_heads(queries, keys, values, step_of)
        return on_device_blocks(queries, keys, values, step_of)

    return jax.shard_map(
        on_device,
        mesh=mesh,
        in_specs=placed,
        out_specs=P(("groups", "pb", "ka"), None),
        check_vma=False,
    )
```

```python
import functools
import math

import jax
import jax.numpy as jnp
from jax import lax
from jax.experimental import pallas as pl
from jax.experimental.pallas import tpu as pltpu
from jax.sharding import PartitionSpec as P

HEAD_DIM = 128


LOW_SCORE = -1e30


def attend_half(q_rows, q_steps, keys_all, values_all, key_steps, block_keys):
    row_count, width = q_rows.shape
    head_size = HEAD_DIM
    head_count = width // head_size
    key_count = keys_all.shape[0]
    block_count = key_count // block_keys
    factor_scale = 1.0 / math.sqrt(head_size)
    q_heads = q_rows.reshape(row_count, head_count, head_size)
    blocks = (
        keys_all.reshape(block_count, block_keys, head_count, head_size),
        values_all.reshape(block_count, block_keys, head_count, head_size),
        key_steps.reshape(block_count, block_keys),
    )
    last_step = q_steps[row_count - 1]

    def compute(carry, key_block, value_block, step_block):
        run_max, run_sum, run_out = carry
        scores = (
            jnp.einsum("rhd,khd->hkr", q_heads, key_block, preferred_element_type=jnp.float32)
            * factor_scale
        )
        visible = step_block[None, :, None] <= q_steps[None, None, :]
        masked = jnp.where(visible, scores, LOW_SCORE)
        new_max = jnp.maximum(run_max, jnp.max(masked, axis=1))
        weights = jnp.where(visible, jnp.exp(masked - new_max[:, None, :]), 0.0)
        rescale = jnp.exp(run_max - new_max)
        new_sum = run_sum * rescale + jnp.sum(weights, axis=1)
        update = jnp.einsum(
            "hkr,khd->rhd",
            weights.astype(jnp.bfloat16),
            value_block,
            preferred_element_type=jnp.float32,
        )
        new_out = run_out * jnp.transpose(rescale)[:, :, None] + update
        return (new_max, new_sum, new_out)

    def visit(carry, block):
        key_block, value_block, step_block = block
        result = lax.cond(
            step_block[0] <= last_step,
            lambda state: compute(state, key_block, value_block, step_block),
            lambda state: state,
            carry,
        )
        return (result, None)

    initial = (
        jnp.full((head_count, row_count), LOW_SCORE, jnp.float32),
        jnp.zeros((head_count, row_count), jnp.float32),
        jnp.zeros((row_count, head_count, head_size), jnp.float32),
    )
    final_state, unused = lax.scan(visit, initial, blocks)
    return final_state


def on_device_blocks(queries, keys, values, step_of):
    block_rows, width = queries.shape
    head_size = HEAD_DIM
    head_count = width // head_size
    key_parts = lax.axis_size("ka")
    query_index = lax.axis_index("pb")
    key_index = lax.axis_index("ka")
    shard_rows = block_rows // key_parts
    half_rows = block_rows // 2
    key_count = keys.shape[0]
    first_steps = lax.dynamic_slice_in_dim(step_of, query_index * block_rows, half_rows)
    second_steps = lax.dynamic_slice_in_dim(
        step_of, query_index * block_rows + half_rows, half_rows
    )
    keys_mine, values_mine = (keys, values)
    key_steps = lax.dynamic_slice_in_dim(step_of, key_index * key_count, key_count)
    keys_all, values_all = (
        lax.all_gather(keys_mine, "pb", axis=1, tiled=True),
        lax.all_gather(values_mine, "pb", axis=1, tiled=True),
    )
    block_keys = math.gcd(64, key_count)
    first_state = attend_half(
        queries[:half_rows], first_steps, keys_all, values_all, key_steps, block_keys
    )
    second_state = attend_half(
        queries[half_rows:], second_steps, keys_all, values_all, key_steps, block_keys
    )
    row_max = jnp.concatenate([first_state[0], second_state[0]], axis=1)
    row_sum = jnp.concatenate([first_state[1], second_state[1]], axis=1)
    row_out = jnp.concatenate([first_state[2], second_state[2]], axis=0)
    sent = (
        jnp.transpose(row_max)[:, None, :],
        jnp.transpose(row_sum)[:, None, :],
        row_out.reshape(block_rows, 1, width),
    )
    got_max, got_sum, got_out = (
        lax.all_to_all(sent[0], "ka", split_axis=0, concat_axis=1, tiled=True),
        lax.all_to_all(sent[1], "ka", split_axis=0, concat_axis=1, tiled=True),
        lax.all_to_all(sent[2], "ka", split_axis=0, concat_axis=1, tiled=True),
    )
    best = jnp.max(got_max, axis=1, keepdims=True)
    weight = jnp.exp(got_max - best)
    total = jnp.sum(got_sum * weight, axis=1)
    shares = weight / total[:, None, :]
    pieces = got_out.reshape(shard_rows, key_parts, head_count, head_size) * shares[:, :, :, None]
    result = jnp.sum(pieces, axis=1).reshape(shard_rows, width)
    result = result.astype(jnp.bfloat16)
    return result


PARTS = 4
MESH = pl.DeviceIdType.MESH


def head_kernel(
    q_ref, k_ref, v_ref, step_ref, out_ref,
    qbuf, kbuf, vbuf, obuf, pbuf, held, held_lse, part_out, part_in, lse_out, lse_in, step_buf,
    q_send, k_send, v_send, o_send, part_send, lse_send,
    q_recv, k_recv, v_recv, o_recv, part_recv, lse_recv, step_sem,
    ready, entered_q, entered_k,
):
    head_size = HEAD_DIM
    parts_q = parts_k = PARTS
    p, a = lax.axis_index("pb"), lax.axis_index("ka")
    me = p * parts_k + a
    q_rows, k_rows = q_ref.shape[0], k_ref.shape[0]
    o_rows = out_ref.shape[0]
    seq = qbuf.shape[1]
    half = seq // 2
    block = 2 * o_rows
    factor = math.log2(math.e) / math.sqrt(head_size)
    barrier = pltpu.get_barrier_semaphore()

    def signal(sem, to_p, to_a):
        pl.semaphore_signal(
            sem, inc=1, device_id={"pb": to_p, "ka": to_a}, device_id_type=MESH
        )

    for other in range(1, parts_k):
        @pl.when(other > a)
        def _():
            signal(barrier, p, other)

    for other in range(1, parts_q):
        @pl.when(jnp.logical_and(a == 0, other > p))
        def _():
            signal(barrier, other, 0)

    @pl.when(a > 0)
    def _():
        pl.semaphore_wait(barrier, a)

    for other in range(parts_k - 1):
        @pl.when(other < a)
        def _():
            signal(entered_k.at[a], p, other)

    def head_columns(index):
        return pl.ds(pl.multiple_of(index * head_size, head_size), head_size)

    q_place = pl.ds(pl.multiple_of(p * q_rows, q_rows), q_rows)

    def keys_of(layer, local, slot):
        place = slice(layer * k_rows, (layer + 1) * k_rows)
        column = slice(local * head_size, (local + 1) * head_size)
        for source, target, sem in ((k_ref, kbuf, k_recv), (v_ref, vbuf, v_recv)):
            pltpu.make_async_copy(
                source.at[:, column], target.at[slot, place], sem.at[slot, layer]
            ).start()

    def send_keys(layer, local, slot, to, rows=None):
        rows = k_rows if rows is None else rows
        place = slice(layer * k_rows, layer * k_rows + rows)
        column = slice(local * head_size, (local + 1) * head_size)
        for source, target, sent, sem in (
            (k_ref, kbuf, k_send, k_recv), (v_ref, vbuf, v_send, v_recv)
        ):
            pltpu.make_async_remote_copy(
                src_ref=source.at[:rows, column], dst_ref=target.at[slot, place],
                send_sem=sent.at[local], recv_sem=sem.at[slot, layer],
                device_id={"pb": p, "ka": to}, device_id_type=MESH,
            ).start()

    def wait_keys_sent(local, rows):
        for source, sent in ((kbuf, k_send), (vbuf, v_send)):
            piece = source.at[0, :rows]
            pltpu.make_async_copy(piece, piece, sent.at[local]).wait()

    @pl.when(a == 0)
    def _():
        keys_of(0, 0, 0)
        pl.semaphore_wait(entered_k.at[1], 1)
        send_keys(0, 1, 0, 1)
        pl.semaphore_wait(entered_k.at[3], 1)
        send_keys(0, 3, 0, 3)
        send_keys(0, 2, 1, 1)
        pl.semaphore_wait(entered_k.at[2], 1)

    @pl.when(a == 1)
    def _():
        keys_of(1, 1, 0)
        keys_of(1, 2, 1)
        send_keys(1, 0, 0, 0)
        pl.semaphore_wait(entered_k.at[3], 1)
        send_keys(1, 3, 0, 3)
        pl.semaphore_wait(entered_k.at[2], 1)

    @pl.when(a == 2)
    def _():
        keys_of(2, 1, 0)
        keys_of(2, 2, 1)
        send_keys(2, 0, 0, 0)
        send_keys(2, 1, 0, 1, o_rows)
        pl.semaphore_wait(entered_k.at[3], 1)
        send_keys(2, 3, 0, 3)
        send_keys(2, 2, 1, 1, o_rows)

    @pl.when(a == 3)
    def _():
        keys_of(3, 3, 0)
        send_keys(3, 1, 0, 2)
        send_keys(3, 0, 0, 0)
        send_keys(3, 2, 1, 2)

    step_copy = pltpu.make_async_copy(step_ref, step_buf, step_sem)
    step_copy.start()

    split = jnp.logical_or(a == 1, a == 2)
    sends_q = jnp.logical_or(a != 2, p >= parts_q // 2)

    @pl.when(a == 0)
    def _():
        @pl.when(p > 0)
        def _():
            pl.semaphore_wait(barrier, p)

        for other in range(parts_q - 1):
            @pl.when(other < p)
            def _():
                signal(entered_q.at[p], other, 0)

        for other in range(parts_q):
            @pl.when(p != other)
            def _():
                @pl.when(other > p)
                def _():
                    pl.semaphore_wait(entered_q.at[other], 1)

                signal(ready.at[p], other, 0)

    for other in range(parts_q):
        @pl.when(p != other)
        def _():
            pl.semaphore_wait(ready.at[other], 1)

            @pl.when(a == 0)
            def _():
                for layer in range(1, parts_k):
                    signal(ready.at[other], p, layer)

    def send_queries(slot, local):
        for to in reversed(range(parts_q)):
            source = q_ref.at[:, head_columns(to * parts_k + local)]

            @pl.when(p != to)
            def _():
                pltpu.make_async_remote_copy(
                    src_ref=source, dst_ref=qbuf.at[slot, q_place],
                    send_sem=q_send.at[slot, to], recv_sem=q_recv.at[slot, p],
                    device_id={"pb": to, "ka": a}, device_id_type=MESH,
                ).start()

            @pl.when(p == to)
            def _():
                pltpu.make_async_copy(
                    source, qbuf.at[slot, q_place], q_recv.at[slot, p]
                ).start()

    @pl.when(sends_q)
    def _():
        send_queries(0, jnp.where(split, 1, a))

    @pl.when(jnp.logical_and(sends_q, split))
    def _():
        send_queries(1, 2)

    step_copy.wait()
    steps = step_buf[...].astype(jnp.float32)
    def arrived(piece, sem):
        pltpu.make_async_copy(piece, piece, sem).wait()

    def queries_in(slot, part):
        arrived(qbuf.at[slot, part * q_rows:(part + 1) * q_rows], q_recv.at[slot, part])

    def keys_in(slot, layer, rows=None):
        rows = k_rows if rows is None else rows
        place = slice(layer * k_rows, layer * k_rows + rows)
        arrived(kbuf.at[slot, place], k_recv.at[slot, layer])
        arrived(vbuf.at[slot, place], v_recv.at[slot, layer])

    def attend(slot, start, low, middle, high):
        stop = start + block
        q_block = qbuf[slot, start:stop, :]
        pieces = [(one, two) for one, two in ((low, middle), (middle, high)) if two > one]
        scores = []
        for one, two in pieces:
            score = lax.dot_general(
                q_block, kbuf[slot, one:two, :], (((1,), (1,)), ((), ())),
                preferred_element_type=jnp.float32,
            )
            if one >= middle:
                q_steps = jnp.concatenate(
                    [
                        jnp.transpose(jnp.broadcast_to(steps[:, row:row + 128], (128, 128)))
                        for row in range(start, stop, 128)
                    ],
                    axis=0,
                )
                visible = jnp.concatenate(
                    [steps[:, row:row + 128] <= q_steps for row in range(one, two, 128)],
                    axis=1,
                )
                score = jnp.where(visible, score, LOW_SCORE)
            scores.append(score)
        row_max = jnp.max(scores[0], axis=1, keepdims=True)
        for score in scores[1:]:
            row_max = jnp.maximum(row_max, jnp.max(score, axis=1, keepdims=True))
        total = None
        for (one, two), score in zip(pieces, scores):
            weights = jnp.exp2((score - row_max) * factor)
            part = jnp.sum(weights, axis=1, keepdims=True)
            pbuf[start:stop, one:two] = weights.astype(jnp.bfloat16)
            total = part if total is None else total + part
        mixed = jnp.dot(
            pbuf[start:stop, low:high], vbuf[slot, low:high, :],
            preferred_element_type=jnp.float32,
        )
        return mixed / total, row_max * factor + jnp.log2(total)

    def deliver(slot, head, start, result):
        obuf[slot, start:start + block, :] = result.astype(jnp.bfloat16)
        for shard in range(start // o_rows, (start + block) // o_rows):
            source = obuf.at[slot, shard * o_rows:(shard + 1) * o_rows]
            target = out_ref.at[:, head_columns(head)]

            @pl.when(me == shard)
            def _():
                pltpu.make_async_copy(source, target, o_recv.at[head]).start()

            @pl.when(me != shard)
            def _():
                pltpu.make_async_remote_copy(
                    src_ref=source, dst_ref=target,
                    send_sem=o_send.at[slot, shard], recv_sem=o_recv.at[head],
                    device_id={"pb": shard // parts_k, "ka": shard % parts_k},
                    device_id_type=MESH,
                ).start()

    def delivered(slot, starts):
        for start in starts:
            for shard in range(start // o_rows, (start + block) // o_rows):
                @pl.when(me != shard)
                def _():
                    arrived(
                        obuf.at[slot, shard * o_rows:(shard + 1) * o_rows],
                        o_send.at[slot, shard],
                    )

    def part_copies(slot, index, to):
        return [
            pltpu.make_async_remote_copy(
                src_ref=source.at[slot, index], dst_ref=target.at[slot, index],
                send_sem=sent.at[slot, index], recv_sem=sem.at[slot, index],
                device_id={"pb": p, "ka": to}, device_id_type=MESH,
            )
            for source, target, sent, sem in (
                (part_out, part_in, part_send, part_recv), (lse_out, lse_in, lse_send, lse_recv)
            )
        ]

    def pass_on(slot, index, to, result, lse):
        part_out[slot, index] = result.astype(jnp.bfloat16)
        for i in range(block // 128):
            row = jnp.transpose(jnp.broadcast_to(lse[i * 128:(i + 1) * 128], (128, 128)))
            lse_out[slot, index, i:i + 1, :] = row[:1]
        for copy in part_copies(slot, index, to):
            copy.start()

    def hold(slot, index, result, lse):
        held[slot, index] = result
        held_lse[slot, index] = jnp.broadcast_to(lse, (block, 128))

    def merged(slot, index, to):
        for copy in part_copies(slot, index, to):
            copy.wait_recv()
        other_lse = jnp.concatenate(
            [
                jnp.transpose(
                    jnp.broadcast_to(lse_in[slot, index, i:i + 1, :], (128, 128))
                )
                for i in range(block // 128)
            ],
            axis=0,
        )
        mine_lse = held_lse[slot, index]
        best = jnp.maximum(mine_lse, other_lse)
        mine, other = jnp.exp2(mine_lse - best), jnp.exp2(other_lse - best)
        both = held[slot, index] * mine + part_in[slot, index].astype(jnp.float32) * other
        return both / (mine + other)

    low_side = [half, half + 2 * block]
    high_side = [half + block, half + 3 * block]

    @pl.when(jnp.logical_not(split))
    def _():
        have_q = have_k = 0
        for start in range(0, seq, block):
            stop = start + block
            high = min(stop + 128, seq)
            while have_q * q_rows < stop:
                queries_in(0, have_q)
                have_q += 1
            while have_k * k_rows < high:
                keys_in(0, have_k)
                have_k += 1
            result, unused = attend(0, start, 0, start, high)
            deliver(0, p * parts_k + a, start, result)
        delivered(0, range(0, seq, block))

    @pl.when(a == 1)
    def _():
        def one_head(slot, carry):
            head = p * parts_k + 1 + slot
            keys_in(slot, 1)
            for part in (2, 3):
                queries_in(slot, part)
            keys_in(slot, 0)
            for index, start in enumerate(high_side):
                pass_on(slot, index, 2, *attend(slot, start, 0, half, half))
            for part in (0, 1):
                queries_in(slot, part)
            keys_in(slot, 2, o_rows)
            for start in (3 * block, block, 2 * block, 0):
                result, unused = attend(slot, start, 0, start, start + block + 128)
                deliver(slot, head, start, result)
            for index, start in enumerate(low_side):
                hold(slot, index, *attend(slot, start, 0, half, half))
            return carry

        def merge_head(slot, carry):
            head = p * parts_k + 1 + slot
            for index, start in enumerate(low_side):
                deliver(slot, head, start, merged(slot, index, 2))
            return carry

        def next_head(slot, carry):
            one_head(slot, carry)

            @pl.when(slot > 0)
            def _():
                merge_head(slot - 1, carry)

            return carry

        lax.fori_loop(0, 2, next_head, 0)
        merge_head(2 - 1, 0)
        for slot in range(2):
            for index in range(2):
                for copy in part_copies(slot, index, 2):
                    copy.wait_send()
            delivered(slot, [*range(0, half, block), *low_side])

    @pl.when(a == 2)
    def _():
        def one_head(slot, carry):
            keys_in(slot, 2)
            queries_in(slot, 2)
            queries_in(slot, 3)
            keys_in(slot, 3)
            for index, start in enumerate(low_side):
                pass_on(slot, index, 1, *attend(slot, start, half, start, start + block + 128))
            for index, start in enumerate(high_side):
                high = min(start + block + 128, seq)
                hold(slot, index, *attend(slot, start, half, start, high))
            return carry

        def merge_head(slot, carry):
            head = p * parts_k + 1 + slot
            for index, start in enumerate(high_side):
                deliver(slot, head, start, merged(slot, index, 1))
            return carry

        lax.fori_loop(0, 2, one_head, 0)
        lax.fori_loop(0, 2, merge_head, 0)
        for slot in range(2):
            for index in range(2):
                for copy in part_copies(slot, index, 1):
                    copy.wait_send()
            delivered(slot, high_side)

    for layer, sent in enumerate((
        ((1, k_rows), (3, k_rows), (2, k_rows)),
        ((3, k_rows), (0, k_rows)),
        ((0, k_rows), (1, o_rows), (3, k_rows), (2, o_rows)),
        ((1, k_rows), (0, k_rows), (2, k_rows)),
    )):
        @pl.when(a == layer)
        def _():
            for local, rows in sent:
                wait_keys_sent(local, rows)

    def wait_queries_sent(slot):
        for to in range(parts_q):
            @pl.when(p != to)
            def _():
                arrived(qbuf.at[slot, :q_rows], q_send.at[slot, to])

    @pl.when(sends_q)
    def _():
        wait_queries_sent(0)

    @pl.when(jnp.logical_and(sends_q, split))
    def _():
        wait_queries_sent(1)

    for head in range(parts_q * parts_k):
        arrived(out_ref.at[:, head * head_size:(head + 1) * head_size], o_recv.at[head])


def on_device_heads(queries, keys, values, step_of):
    block_rows, width = queries.shape
    seq = step_of.shape[0]
    shard_rows = block_rows // PARTS
    block = 2 * shard_rows
    buffer = pltpu.VMEM((2, seq, HEAD_DIM), jnp.bfloat16)
    anywhere = pl.BlockSpec(memory_space=pltpu.HBM)
    dma = pltpu.SemaphoreType.DMA
    return pl.pallas_call(
        head_kernel,
        out_shape=jax.ShapeDtypeStruct((shard_rows, width), jnp.bfloat16),
        in_specs=[anywhere, anywhere, anywhere, anywhere],
        out_specs=pl.BlockSpec(memory_space=pltpu.VMEM),
        scratch_shapes=[
            buffer, buffer, buffer, buffer,
            pltpu.VMEM((seq, seq), jnp.bfloat16),
            pltpu.VMEM((2, 2, block, HEAD_DIM), jnp.float32),
            pltpu.VMEM((2, 2, block, HEAD_DIM), jnp.float32),
            pltpu.VMEM((2, 2, block, HEAD_DIM), jnp.bfloat16),
            pltpu.VMEM((2, 2, block, HEAD_DIM), jnp.bfloat16),
            pltpu.VMEM((2, 2, 8, 128), jnp.float32),
            pltpu.VMEM((2, 2, 8, 128), jnp.float32),
            pltpu.VMEM((1, seq), jnp.int32),
            dma((2, PARTS)), dma((PARTS,)), dma((PARTS,)), dma((2, PARTS * PARTS)),
            dma((2, 2)), dma((2, 2)),
            dma((2, PARTS)), dma((2, PARTS)), dma((2, PARTS)), dma((PARTS * PARTS,)),
            dma((2, 2)), dma((2, 2)), dma,
            pltpu.SemaphoreType.REGULAR((PARTS,)),
            pltpu.SemaphoreType.REGULAR((PARTS,)),
            pltpu.SemaphoreType.REGULAR((PARTS,)),
        ],
        compiler_params=pltpu.CompilerParams(
            collective_id=0, has_side_effects=True, vmem_limit_bytes=48 * 1024 * 1024
        ),
    )(*[
        pltpu.with_memory_space_constraint(array, pltpu.HBM)
        for array in (queries, keys, values, step_of.reshape(1, seq))
    ])


def head_per_device(mesh_shape, queries, keys, step_of):
    return (
        mesh_shape["pb"] == PARTS
        and mesh_shape["ka"] == PARTS
        and keys.shape[1] == PARTS * HEAD_DIM
        and step_of.shape[0] == PARTS * PARTS * 128
    )


def solution(mesh):
    placed = (
        P(("groups", "pb"), None),
        P(("groups", "ka"), "pb"),
        P(("groups", "ka"), "pb"),
        P("groups"),
    )

    def on_device(queries, keys, values, step_of):
        if head_per_device(mesh.shape, queries, keys, step_of):
            return on_device_heads(queries, keys, values, step_of)
        return on_device_blocks(queries, keys, values, step_of)

    return jax.shard_map(
        on_device,
        mesh=mesh,
        in_specs=placed,
        out_specs=P(("groups", "pb", "ka"), None),
        check_vma=False,
    )
```

```python
import functools
import math

import jax
import jax.numpy as jnp
from jax import lax
from jax.experimental import pallas as pl
from jax.experimental.pallas import tpu as pltpu
from jax.sharding import PartitionSpec as P

HEAD_DIM = 128


LOW_SCORE = -1e30


def attend_half(q_rows, q_steps, keys_all, values_all, key_steps, block_keys):
    row_count, width = q_rows.shape
    head_size = HEAD_DIM
    head_count = width // head_size
    key_count = keys_all.shape[0]
    block_count = key_count // block_keys
    factor_scale = 1.0 / math.sqrt(head_size)
    q_heads = q_rows.reshape(row_count, head_count, head_size)
    blocks = (
        keys_all.reshape(block_count, block_keys, head_count, head_size),
        values_all.reshape(block_count, block_keys, head_count, head_size),
        key_steps.reshape(block_count, block_keys),
    )
    last_step = q_steps[row_count - 1]

    def compute(carry, key_block, value_block, step_block):
        run_max, run_sum, run_out = carry
        scores = (
            jnp.einsum("rhd,khd->hkr", q_heads, key_block, preferred_element_type=jnp.float32)
            * factor_scale
        )
        visible = step_block[None, :, None] <= q_steps[None, None, :]
        masked = jnp.where(visible, scores, LOW_SCORE)
        new_max = jnp.maximum(run_max, jnp.max(masked, axis=1))
        weights = jnp.where(visible, jnp.exp(masked - new_max[:, None, :]), 0.0)
        rescale = jnp.exp(run_max - new_max)
        new_sum = run_sum * rescale + jnp.sum(weights, axis=1)
        update = jnp.einsum(
            "hkr,khd->rhd",
            weights.astype(jnp.bfloat16),
            value_block,
            preferred_element_type=jnp.float32,
        )
        new_out = run_out * jnp.transpose(rescale)[:, :, None] + update
        return (new_max, new_sum, new_out)

    def visit(carry, block):
        key_block, value_block, step_block = block
        result = lax.cond(
            step_block[0] <= last_step,
            lambda state: compute(state, key_block, value_block, step_block),
            lambda state: state,
            carry,
        )
        return (result, None)

    initial = (
        jnp.full((head_count, row_count), LOW_SCORE, jnp.float32),
        jnp.zeros((head_count, row_count), jnp.float32),
        jnp.zeros((row_count, head_count, head_size), jnp.float32),
    )
    final_state, unused = lax.scan(visit, initial, blocks)
    return final_state


def on_device_blocks(queries, keys, values, step_of):
    block_rows, width = queries.shape
    head_size = HEAD_DIM
    head_count = width // head_size
    key_parts = lax.axis_size("ka")
    query_index = lax.axis_index("pb")
    key_index = lax.axis_index("ka")
    shard_rows = block_rows // key_parts
    half_rows = block_rows // 2
    key_count = keys.shape[0]
    first_steps = lax.dynamic_slice_in_dim(step_of, query_index * block_rows, half_rows)
    second_steps = lax.dynamic_slice_in_dim(
        step_of, query_index * block_rows + half_rows, half_rows
    )
    keys_mine, values_mine = (keys, values)
    key_steps = lax.dynamic_slice_in_dim(step_of, key_index * key_count, key_count)
    keys_all, values_all = (
        lax.all_gather(keys_mine, "pb", axis=1, tiled=True),
        lax.all_gather(values_mine, "pb", axis=1, tiled=True),
    )
    block_keys = math.gcd(64, key_count)
    first_state = attend_half(
        queries[:half_rows], first_steps, keys_all, values_all, key_steps, block_keys
    )
    second_state = attend_half(
        queries[half_rows:], second_steps, keys_all, values_all, key_steps, block_keys
    )
    row_max = jnp.concatenate([first_state[0], second_state[0]], axis=1)
    row_sum = jnp.concatenate([first_state[1], second_state[1]], axis=1)
    row_out = jnp.concatenate([first_state[2], second_state[2]], axis=0)
    sent = (
        jnp.transpose(row_max)[:, None, :],
        jnp.transpose(row_sum)[:, None, :],
        row_out.reshape(block_rows, 1, width),
    )
    got_max, got_sum, got_out = (
        lax.all_to_all(sent[0], "ka", split_axis=0, concat_axis=1, tiled=True),
        lax.all_to_all(sent[1], "ka", split_axis=0, concat_axis=1, tiled=True),
        lax.all_to_all(sent[2], "ka", split_axis=0, concat_axis=1, tiled=True),
    )
    best = jnp.max(got_max, axis=1, keepdims=True)
    weight = jnp.exp(got_max - best)
    total = jnp.sum(got_sum * weight, axis=1)
    shares = weight / total[:, None, :]
    pieces = got_out.reshape(shard_rows, key_parts, head_count, head_size) * shares[:, :, :, None]
    result = jnp.sum(pieces, axis=1).reshape(shard_rows, width)
    result = result.astype(jnp.bfloat16)
    return result


PARTS = 4
MESH = pl.DeviceIdType.MESH


def head_kernel(
    q_ref, k_ref, v_ref, step_ref, out_ref,
    qbuf, kbuf, vbuf, obuf, pbuf, held, held_lse, part_out, part_in, lse_out, lse_in, step_buf,
    q_send, k_send, v_send, o_send, part_send, lse_send,
    q_recv, k_recv, v_recv, o_recv, part_recv, lse_recv, step_sem,
    ready, entered_q, entered_k,
):
    head_size = HEAD_DIM
    parts_q = parts_k = PARTS
    p, a = lax.axis_index("pb"), lax.axis_index("ka")
    me = p * parts_k + a
    q_rows, k_rows = q_ref.shape[0], k_ref.shape[0]
    o_rows = out_ref.shape[0]
    seq = qbuf.shape[1]
    half = seq // 2
    block = 2 * o_rows
    factor = math.log2(math.e) / math.sqrt(head_size)
    barrier = pltpu.get_barrier_semaphore()

    def signal(sem, to_p, to_a):
        pl.semaphore_signal(
            sem, inc=1, device_id={"pb": to_p, "ka": to_a}, device_id_type=MESH
        )

    for other in range(1, parts_k):
        @pl.when(other > a)
        def _():
            signal(barrier, p, other)

    for other in range(1, parts_q):
        @pl.when(jnp.logical_and(a == 0, other > p))
        def _():
            signal(barrier, other, 0)

    @pl.when(a > 0)
    def _():
        pl.semaphore_wait(barrier, a)

    for other in range(parts_k - 1):
        @pl.when(other < a)
        def _():
            signal(entered_k.at[a], p, other)

    def head_columns(index):
        return pl.ds(pl.multiple_of(index * head_size, head_size), head_size)

    q_place = pl.ds(pl.multiple_of(p * q_rows, q_rows), q_rows)

    def keys_of(layer, local, slot):
        place = slice(layer * k_rows, (layer + 1) * k_rows)
        column = slice(local * head_size, (local + 1) * head_size)
        for source, target, sem in ((k_ref, kbuf, k_recv), (v_ref, vbuf, v_recv)):
            pltpu.make_async_copy(
                source.at[:, column], target.at[slot, place], sem.at[slot, layer]
            ).start()

    def send_keys(layer, local, slot, to, rows=None):
        rows = k_rows if rows is None else rows
        place = slice(layer * k_rows, layer * k_rows + rows)
        column = slice(local * head_size, (local + 1) * head_size)
        for source, target, sent, sem in (
            (k_ref, kbuf, k_send, k_recv), (v_ref, vbuf, v_send, v_recv)
        ):
            pltpu.make_async_remote_copy(
                src_ref=source.at[:rows, column], dst_ref=target.at[slot, place],
                send_sem=sent.at[local], recv_sem=sem.at[slot, layer],
                device_id={"pb": p, "ka": to}, device_id_type=MESH,
            ).start()

    def wait_keys_sent(local, rows):
        for source, sent in ((kbuf, k_send), (vbuf, v_send)):
            piece = source.at[0, :rows]
            pltpu.make_async_copy(piece, piece, sent.at[local]).wait()

    @pl.when(a == 0)
    def _():
        keys_of(0, 0, 0)
        pl.semaphore_wait(entered_k.at[1], 1)
        send_keys(0, 1, 0, 1)
        pl.semaphore_wait(entered_k.at[3], 1)
        send_keys(0, 3, 0, 3)
        send_keys(0, 2, 1, 1)
        pl.semaphore_wait(entered_k.at[2], 1)

    @pl.when(a == 1)
    def _():
        send_keys(1, 0, 0, 0)
        keys_of(1, 1, 0)
        keys_of(1, 2, 1)
        pl.semaphore_wait(entered_k.at[3], 1)
        send_keys(1, 3, 0, 3)
        pl.semaphore_wait(entered_k.at[2], 1)

    @pl.when(a == 2)
    def _():
        keys_of(2, 2, 1)
        send_keys(2, 0, 0, 0)
        keys_of(2, 1, 0)
        send_keys(2, 1, 0, 1, o_rows)
        pl.semaphore_wait(entered_k.at[3], 1)
        send_keys(2, 3, 0, 3)
        send_keys(2, 2, 1, 1, o_rows)

    @pl.when(a == 3)
    def _():
        keys_of(3, 3, 0)
        send_keys(3, 1, 0, 2)
        send_keys(3, 0, 0, 0)
        send_keys(3, 2, 1, 2)

    step_copy = pltpu.make_async_copy(step_ref, step_buf, step_sem)
    step_copy.start()

    split = jnp.logical_or(a == 1, a == 2)
    sends_q = jnp.logical_or(a != 2, p >= parts_q // 2)

    @pl.when(a == 0)
    def _():
        @pl.when(p > 0)
        def _():
            pl.semaphore_wait(barrier, p)

        for other in range(parts_q - 1):
            @pl.when(other < p)
            def _():
                signal(entered_q.at[p], other, 0)

        for other in range(parts_q):
            @pl.when(p != other)
            def _():
                @pl.when(other > p)
                def _():
                    pl.semaphore_wait(entered_q.at[other], 1)

                signal(ready.at[p], other, 0)

    for other in range(parts_q):
        @pl.when(p != other)
        def _():
            pl.semaphore_wait(ready.at[other], 1)

            @pl.when(a == 0)
            def _():
                for layer in range(1, parts_k):
                    signal(ready.at[other], p, layer)

    def send_queries(slot, local):
        for to in reversed(range(parts_q)):
            source = q_ref.at[:, head_columns(to * parts_k + local)]

            @pl.when(p != to)
            def _():
                pltpu.make_async_remote_copy(
                    src_ref=source, dst_ref=qbuf.at[slot, q_place],
                    send_sem=q_send.at[slot, to], recv_sem=q_recv.at[slot, p],
                    device_id={"pb": to, "ka": a}, device_id_type=MESH,
                ).start()

            @pl.when(p == to)
            def _():
                pltpu.make_async_copy(
                    source, qbuf.at[slot, q_place], q_recv.at[slot, p]
                ).start()

    @pl.when(sends_q)
    def _():
        send_queries(0, jnp.where(split, 1, a))

    @pl.when(jnp.logical_and(sends_q, split))
    def _():
        send_queries(1, 2)

    step_copy.wait()
    steps = step_buf[...].astype(jnp.float32)
    def arrived(piece, sem):
        pltpu.make_async_copy(piece, piece, sem).wait()

    def queries_in(slot, part):
        arrived(qbuf.at[slot, part * q_rows:(part + 1) * q_rows], q_recv.at[slot, part])

    def keys_in(slot, layer, rows=None):
        rows = k_rows if rows is None else rows
        place = slice(layer * k_rows, layer * k_rows + rows)
        arrived(kbuf.at[slot, place], k_recv.at[slot, layer])
        arrived(vbuf.at[slot, place], v_recv.at[slot, layer])

    def attend(slot, start, low, middle, high):
        stop = start + block
        q_block = qbuf[slot, start:stop, :]
        pieces = [(one, two) for one, two in ((low, middle), (middle, high)) if two > one]
        scores = []
        for one, two in pieces:
            score = lax.dot_general(
                q_block, kbuf[slot, one:two, :], (((1,), (1,)), ((), ())),
                preferred_element_type=jnp.float32,
            )
            if one >= middle:
                q_steps = jnp.concatenate(
                    [
                        jnp.transpose(jnp.broadcast_to(steps[:, row:row + 128], (128, 128)))
                        for row in range(start, stop, 128)
                    ],
                    axis=0,
                )
                visible = jnp.concatenate(
                    [steps[:, row:row + 128] <= q_steps for row in range(one, two, 128)],
                    axis=1,
                )
                score = jnp.where(visible, score, LOW_SCORE)
            scores.append(score)
        row_max = jnp.max(scores[0], axis=1, keepdims=True)
        for score in scores[1:]:
            row_max = jnp.maximum(row_max, jnp.max(score, axis=1, keepdims=True))
        total = None
        for (one, two), score in zip(pieces, scores):
            weights = jnp.exp2((score - row_max) * factor)
            part = jnp.sum(weights, axis=1, keepdims=True)
            pbuf[start:stop, one:two] = weights.astype(jnp.bfloat16)
            total = part if total is None else total + part
        mixed = jnp.dot(
            pbuf[start:stop, low:high], vbuf[slot, low:high, :],
            preferred_element_type=jnp.float32,
        )
        return mixed / total, row_max * factor + jnp.log2(total)

    def deliver(slot, head, start, result):
        obuf[slot, start:start + block, :] = result.astype(jnp.bfloat16)
        for shard in range(start // o_rows, (start + block) // o_rows):
            source = obuf.at[slot, shard * o_rows:(shard + 1) * o_rows]
            target = out_ref.at[:, head_columns(head)]

            @pl.when(me == shard)
            def _():
                pltpu.make_async_copy(source, target, o_recv.at[head]).start()

            @pl.when(me != shard)
            def _():
                pltpu.make_async_remote_copy(
                    src_ref=source, dst_ref=target,
                    send_sem=o_send.at[slot, shard], recv_sem=o_recv.at[head],
                    device_id={"pb": shard // parts_k, "ka": shard % parts_k},
                    device_id_type=MESH,
                ).start()

    def delivered(slot, starts):
        for start in starts:
            for shard in range(start // o_rows, (start + block) // o_rows):
                @pl.when(me != shard)
                def _():
                    arrived(
                        obuf.at[slot, shard * o_rows:(shard + 1) * o_rows],
                        o_send.at[slot, shard],
                    )

    def part_copies(slot, index, to):
        return [
            pltpu.make_async_remote_copy(
                src_ref=source.at[slot, index], dst_ref=target.at[slot, index],
                send_sem=sent.at[slot, index], recv_sem=sem.at[slot, index],
                device_id={"pb": p, "ka": to}, device_id_type=MESH,
            )
            for source, target, sent, sem in (
                (part_out, part_in, part_send, part_recv), (lse_out, lse_in, lse_send, lse_recv)
            )
        ]

    def pass_on(slot, index, to, result, lse):
        part_out[slot, index] = result.astype(jnp.bfloat16)
        for i in range(block // 128):
            row = jnp.transpose(jnp.broadcast_to(lse[i * 128:(i + 1) * 128], (128, 128)))
            lse_out[slot, index, i:i + 1, :] = row[:1]
        for copy in part_copies(slot, index, to):
            copy.start()

    def hold(slot, index, result, lse):
        held[slot, index] = result
        held_lse[slot, index] = jnp.broadcast_to(lse, (block, 128))

    def merged(slot, index, to):
        for copy in part_copies(slot, index, to):
            copy.wait_recv()
        other_lse = jnp.concatenate(
            [
                jnp.transpose(
                    jnp.broadcast_to(lse_in[slot, index, i:i + 1, :], (128, 128))
                )
                for i in range(block // 128)
            ],
            axis=0,
        )
        mine_lse = held_lse[slot, index]
        best = jnp.maximum(mine_lse, other_lse)
        mine, other = jnp.exp2(mine_lse - best), jnp.exp2(other_lse - best)
        both = held[slot, index] * mine + part_in[slot, index].astype(jnp.float32) * other
        return both / (mine + other)

    low_side = [half, half + 2 * block]
    high_side = [half + block, half + 3 * block]

    @pl.when(jnp.logical_not(split))
    def _():
        have_q = have_k = 0
        for start in range(0, seq, block):
            stop = start + block
            high = min(stop + 128, seq)
            while have_q * q_rows < stop:
                queries_in(0, have_q)
                have_q += 1
            while have_k * k_rows < high:
                keys_in(0, have_k)
                have_k += 1
            result, unused = attend(0, start, 0, start, high)
            deliver(0, p * parts_k + a, start, result)
        delivered(0, range(0, seq, block))

    @pl.when(a == 1)
    def _():
        def one_head(slot, carry):
            head = p * parts_k + 1 + slot
            keys_in(slot, 1)
            for part in (2, 3):
                queries_in(slot, part)
            keys_in(slot, 0)
            for index, start in enumerate(high_side):
                pass_on(slot, index, 2, *attend(slot, start, 0, half, half))
            for part in (0, 1):
                queries_in(slot, part)
            keys_in(slot, 2, o_rows)
            for start in (3 * block, block, 2 * block, 0):
                result, unused = attend(slot, start, 0, start, start + block + 128)
                deliver(slot, head, start, result)
            for index, start in enumerate(low_side):
                hold(slot, index, *attend(slot, start, 0, half, half))
            return carry

        def merge_head(slot, carry):
            head = p * parts_k + 1 + slot
            for index, start in enumerate(low_side):
                deliver(slot, head, start, merged(slot, index, 2))
            return carry

        def next_head(slot, carry):
            one_head(slot, carry)

            @pl.when(slot > 0)
            def _():
                merge_head(slot - 1, carry)

            return carry

        lax.fori_loop(0, 2, next_head, 0)
        merge_head(2 - 1, 0)
        for slot in range(2):
            for index in range(2):
                for copy in part_copies(slot, index, 2):
                    copy.wait_send()
            delivered(slot, [*range(0, half, block), *low_side])

    @pl.when(a == 2)
    def _():
        def one_head(slot, carry):
            keys_in(slot, 2)
            queries_in(slot, 2)
            queries_in(slot, 3)
            keys_in(slot, 3)
            for index, start in enumerate(low_side):
                pass_on(slot, index, 1, *attend(slot, start, half, start, start + block + 128))
            for index, start in enumerate(high_side):
                high = min(start + block + 128, seq)
                hold(slot, index, *attend(slot, start, half, start, high))
            return carry

        def merge_head(slot, carry):
            head = p * parts_k + 1 + slot
            for index, start in enumerate(high_side):
                deliver(slot, head, start, merged(slot, index, 1))
            return carry

        one_head(0, 0)
        merge_head(0, 0)
        one_head(1, 0)
        merge_head(1, 0)
        for slot in range(2):
            for index in range(2):
                for copy in part_copies(slot, index, 1):
                    copy.wait_send()
            delivered(slot, high_side)

    for layer, sent in enumerate((
        ((1, k_rows), (3, k_rows), (2, k_rows)),
        ((3, k_rows), (0, k_rows)),
        ((0, k_rows), (1, o_rows), (3, k_rows), (2, o_rows)),
        ((1, k_rows), (0, k_rows), (2, k_rows)),
    )):
        @pl.when(a == layer)
        def _():
            for local, rows in sent:
                wait_keys_sent(local, rows)

    def wait_queries_sent(slot):
        for to in range(parts_q):
            @pl.when(p != to)
            def _():
                arrived(qbuf.at[slot, :q_rows], q_send.at[slot, to])

    @pl.when(sends_q)
    def _():
        wait_queries_sent(0)

    @pl.when(jnp.logical_and(sends_q, split))
    def _():
        wait_queries_sent(1)

    for head in range(parts_q * parts_k):
        arrived(out_ref.at[:, head * head_size:(head + 1) * head_size], o_recv.at[head])


def on_device_heads(queries, keys, values, step_of):
    block_rows, width = queries.shape
    seq = step_of.shape[0]
    shard_rows = block_rows // PARTS
    block = 2 * shard_rows
    buffer = pltpu.VMEM((2, seq, HEAD_DIM), jnp.bfloat16)
    anywhere = pl.BlockSpec(memory_space=pltpu.HBM)
    dma = pltpu.SemaphoreType.DMA
    return pl.pallas_call(
        head_kernel,
        out_shape=jax.ShapeDtypeStruct((shard_rows, width), jnp.bfloat16),
        in_specs=[anywhere, anywhere, anywhere, anywhere],
        out_specs=pl.BlockSpec(memory_space=pltpu.VMEM),
        scratch_shapes=[
            buffer, buffer, buffer, buffer,
            pltpu.VMEM((seq, seq), jnp.bfloat16),
            pltpu.VMEM((2, 2, block, HEAD_DIM), jnp.float32),
            pltpu.VMEM((2, 2, block, HEAD_DIM), jnp.float32),
            pltpu.VMEM((2, 2, block, HEAD_DIM), jnp.bfloat16),
            pltpu.VMEM((2, 2, block, HEAD_DIM), jnp.bfloat16),
            pltpu.VMEM((2, 2, 8, 128), jnp.float32),
            pltpu.VMEM((2, 2, 8, 128), jnp.float32),
            pltpu.VMEM((1, seq), jnp.int32),
            dma((2, PARTS)), dma((PARTS,)), dma((PARTS,)), dma((2, PARTS * PARTS)),
            dma((2, 2)), dma((2, 2)),
            dma((2, PARTS)), dma((2, PARTS)), dma((2, PARTS)), dma((PARTS * PARTS,)),
            dma((2, 2)), dma((2, 2)), dma,
            pltpu.SemaphoreType.REGULAR((PARTS,)),
            pltpu.SemaphoreType.REGULAR((PARTS,)),
            pltpu.SemaphoreType.REGULAR((PARTS,)),
        ],
        compiler_params=pltpu.CompilerParams(
            collective_id=0, has_side_effects=True, vmem_limit_bytes=48 * 1024 * 1024
        ),
    )(*[
        pltpu.with_memory_space_constraint(array, pltpu.HBM)
        for array in (queries, keys, values, step_of.reshape(1, seq))
    ])


def head_per_device(mesh_shape, queries, keys, step_of):
    return (
        mesh_shape["pb"] == PARTS
        and mesh_shape["ka"] == PARTS
        and keys.shape[1] == PARTS * HEAD_DIM
        and step_of.shape[0] == PARTS * PARTS * 128
    )


def solution(mesh):
    placed = (
        P(("groups", "pb"), None),
        P(("groups", "ka"), "pb"),
        P(("groups", "ka"), "pb"),
        P("groups"),
    )

    def on_device(queries, keys, values, step_of):
        if head_per_device(mesh.shape, queries, keys, step_of):
            return on_device_heads(queries, keys, values, step_of)
        return on_device_blocks(queries, keys, values, step_of)

    return jax.shard_map(
        on_device,
        mesh=mesh,
        in_specs=placed,
        out_specs=P(("groups", "pb", "ka"), None),
        check_vma=False,
    )
```
